32 devices in a mesh: dp: 8 (over z, y), tensor: 4 (over x, core).
Axes of the slice: x: 2, y: 2, z: 4, core: 2. Of those that a mesh axis runs over, the one named last changes fastest.
Arguments:
- hidden_in: bfloat16 [8192, 2048], P('dp'), may hold values from -6 to 6
- doc_ids: int32 [8, 1024], P('dp'), may hold values from 0 to 7, never falling along the last dimension, each value on 1 to 256 neighbouring positions
- ln1_gain: bfloat16 [2048], replicated, may hold values from 0.5 to 1.5
- ln1_bias: bfloat16 [2048], replicated, may hold values from -4 to 4
- q_weight: bfloat16 [2048, 2048], P(None, 'tensor'), may hold values from -0.1875 to 0.1875
- q_bias: bfloat16 [2048], P('tensor'), may hold values from -6 to 6
- kv_weight: bfloat16 [2048, 256], replicated, may hold values from -0.1875 to 0.1875
- v_bias: bfloat16 [128], replicated, may hold values from -6 to 6
- o_weight: bfloat16 [2048, 2048], P('tensor'), may hold values from -0.75 to 0.75
- o_bias: bfloat16 [2048], replicated, may hold values from -4 to 4
- ln2_gain: bfloat16 [2048], replicated, may hold values from 0.5 to 1.5
- ln2_bias: bfloat16 [2048], replicated, may hold values from -4 to 4
- up_weight: bfloat16 [2048, 8192], P(None, 'tensor'), may hold values from -0.125 to 0.125
- up_bias: bfloat16 [8192], P('tensor'), may hold values from -6 to 6
- down_weight: bfloat16 [8192, 2048], P('tensor'), may hold values from -0.09375 to 0.09375
- down_bias: bfloat16 [2048], replicated, may hold values from -4 to 4
- cotangent: bfloat16 [8192, 2048], P('dp'), may hold values from -6 to 6
Outputs:
- layer_out: bfloat16 [8192, 2048], P(('dp', 'tensor'))
- input_grad: float32 [8192, 2048], P('dp')
- ln1_gain_grad: float32 [2048], replicated
- ln1_bias_grad: float32 [2048], replicated
- q_weight_grad: float32 [2048, 2048], P('dp', 'tensor')
- q_bias_grad: float32 [2048], P('tensor')
- kv_weight_grad: float32 [2048, 256], P('dp')
- v_bias_grad: float32 [128], replicated
- o_weight_grad: float32 [2048, 2048], P('tensor', 'dp')
- o_bias_grad: float32 [2048], replicated
- ln2_gain_grad: float32 [2048], replicated
- ln2_bias_grad: float32 [2048], replicated
- up_weight_grad: float32 [2048, 8192], P('dp', 'tensor')
- up_bias_grad: float32 [8192], P('tensor')
- down_weight_grad: float32 [8192, 2048], P('tensor', 'dp')
- down_bias_grad: float32 [2048], replicated
The draws below stay inside these ranges and needn't reach their ends.
Inputs may be any that keep to these rules, and one draw needn't show every extreme that they name: `doc_ids`: within each window the ids never fall, every id from 0 to 7 occurs, each document has at most 256 tokens and one has exactly 256.
All inputs are finite; a program needn't handle non-finite values.
Results may differ from the reference program's by a relative error of at most 0.012.
The reference program's roundings to bfloat16 on the way count: a program that leaves them out, or rounds other values in their place, can miss the bound.
Values sent between devices are 32-bit elements; how exact they have to be, the bound alone decides.
No kernel may reach another device: no remote copies, remote signals or barrier semaphores. Data moves between devices by JAX's collectives and lax.ppermute only.
A program may use at most 256 MiB of HBM per device.

```python
import math
import jax
import jax.numpy as jnp
import numpy as np
from jax import lax

D = 2048
HEADS = 16
HD = 128
FF = 8192
LEN = 1024
WINDOWS = 8
TOKENS = 8192
DOCS = 8
DOC_MOST = 256


def strengthened(entries, stream_key, source, target, blocks, factor):
    owner, partner = [(jnp.arange(entries.shape[dim]) // (entries.shape[dim] // blocks)).reshape([-1 if axis == dim else 1 for axis in range(entries.ndim)]) for dim in (source, target)]
    chosen = jax.random.permutation(stream_key, blocks)[partner]
    strong = (owner == chosen) | (owner == (partner + blocks // 2) % blocks)
    return jnp.where(strong, factor * entries, entries)


def block_scale(rng, extent, shards, low, top_value):
    loudness = 1.0
    for dim, blocks in shards:
        steps = jax.random.uniform(jax.random.fold_in(jax.random.fold_in(rng, 6), dim), (blocks,), jnp.float32, low / len(shards), top_value / len(shards))
        loudness = loudness * jnp.repeat(jnp.exp(steps), extent[dim] // blocks).reshape((-1,) + (1,) * (len(extent) - 1 - dim))
    return loudness


def split_up(amount, total, reach, lean):
    loads = [(1 << 20) // math.isqrt(standing ** lean) + 1 for standing in range(2, amount + 1)]
    spare, holding = total - reach - (amount - 1), [1] * (amount - 1)
    while spare > 0:
        movable = [i for i in range(amount - 1) if holding[i] < reach]
        mass, left = sum([loads[i] for i in movable]), spare
        for i in movable:
            more = min(reach - holding[i], max(1, left * loads[i] // mass), spare)
            holding[i] = holding[i] + more
            spare = spare - more
    return np.array([reach] + holding)


def uneven(own_key, number_of, total, most, skew):
    if number_of == 2:
        one = jax.random.randint(own_key, (), max(1, total - most), min(most, total - 1) + 1)
        return jnp.stack([one, total - one])
    tallies = jnp.asarray(split_up(number_of, total, most, skew), jnp.int32)
    couples = (number_of - 1) // 2
    giver, receiver = tallies[1:1 + 2 * couples:2], tallies[2:2 + 2 * couples:2]
    margin = jnp.minimum(giver - 1, most - receiver)
    shifted = jax.random.randint(jax.random.fold_in(own_key, 1), (couples,), 0, 1 << 20) % (margin + 1)
    tallies = tallies.at[1:1 + 2 * couples:2].set(giver - shifted).at[2:2 + 2 * couples:2].set(receiver + shifted)
    return tallies[jax.random.permutation(jax.random.fold_in(own_key, 2), number_of)]


def bell_draw(stream_key, shape, spread, bound, shards=(), dtype=jnp.bfloat16):
    factor_of = block_scale(stream_key, shape, shards, -0.22, 0.18) if shards else 1.0
    values = jax.random.normal(stream_key, shape, jnp.float32) * spread * factor_of
    return jnp.minimum(jnp.maximum(values, -bound), bound).astype(dtype)


def bell_draw_with(stream_key, shape, spread, reach, cuts, heavy, kind=jnp.bfloat16):
    entries = spread * jax.random.normal(stream_key, shape, jnp.float32)
    if cuts:
        entries = entries * block_scale(stream_key, shape, cuts, -0.22, 0.18)
    return jnp.clip(strengthened(entries, jax.random.fold_in(stream_key, 3), *heavy), -reach, reach).astype(kind)


def setup_inputs(seed: int = 0) -> dict:
    seeds = jax.random.split(jax.random.key(seed), 18)
    hidden_in = bell_draw_with(seeds[0], (TOKENS, D), 1.0, 6.0, ((0, 8),), (0, 1, 8, 2.0))
    doc_ids = jax.vmap(lambda own: jnp.searchsorted(jnp.cumsum(uneven(own, DOCS, LEN, DOC_MOST, 1)), jnp.arange(LEN), side="right"))(jax.random.split(seeds[1], WINDOWS)).reshape((WINDOWS, LEN)).astype(jnp.int32)
    ln1_gain = jnp.clip(1.0 + 0.1 * jax.random.normal(seeds[2], (D,), jnp.float32), 0.5, 1.5).astype(jnp.bfloat16)
    ln1_bias = bell_draw(seeds[3], (D,), 0.3, 4.0)
    q_weight = bell_draw(seeds[4], (D, HEADS * HD), (D // 2) ** -0.5, 0.1875, ((1, 4),))
    q_bias = bell_draw(seeds[5], (HEADS * HD,), 0.5, 6.0, ((0, 4),))
    kv_weight = bell_draw(seeds[6], (D, 2 * HD), (D // 2) ** -0.5, 0.1875)
    v_bias = bell_draw(seeds[7], (HD,), 0.5, 6.0)
    o_weight = bell_draw(seeds[8], (HEADS * HD, D), (HEADS * HD // 32) ** -0.5, 0.75, ((0, 4),))
    o_bias = bell_draw(seeds[9], (D,), 0.3, 4.0)
    ln2_gain = jnp.clip(1.0 + 0.1 * jax.random.normal(seeds[10], (D,), jnp.float32), 0.5, 1.5).astype(jnp.bfloat16)
    ln2_bias = bell_draw(seeds[11], (D,), 0.3, 4.0)
    up_weight = bell_draw(seeds[12], (D, FF), D ** -0.5, 0.125, ((1, 4),))
    up_bias = bell_draw(seeds[13], (FF,), 0.5, 6.0, ((0, 4),))
    down_weight = bell_draw(seeds[14], (FF, D), (FF // 2) ** -0.5, 0.09375, ((0, 4),))
    down_bias = bell_draw(seeds[15], (D,), 0.3, 4.0)
    cotangent = bell_draw_with(seeds[16], (TOKENS, D), 1.0, 6.0, ((0, 8),), (0, 1, 8, 2.0))
    return {"hidden_in": hidden_in, "doc_ids": doc_ids, "ln1_gain": ln1_gain, "ln1_bias": ln1_bias, "q_weight": q_weight, "q_bias": q_bias, "kv_weight": kv_weight, "v_bias": v_bias, "o_weight": o_weight, "o_bias": o_bias, "ln2_gain": ln2_gain, "ln2_bias": ln2_bias, "up_weight": up_weight, "up_bias": up_bias, "down_weight": down_weight, "down_bias": down_bias, "cotangent": cotangent}


EPS = 1e-05
HIGH = lax.Precision.HIGHEST

@jax.custom_vjp
def low(v):
    return lax.optimization_barrier(v.astype(jnp.bfloat16)).astype(jnp.float32)

@jax.custom_vjp
def low_back(v):
    return v

def low_keep(v):
    return (low(v), None)

def low_pass(kept, grad):
    return (grad,)

def back_keep(v):
    return (v, None)

def back_low(kept, grad):
    return (low(grad),)
low.defvjp(low_keep, low_pass)
low_back.defvjp(back_keep, back_low)

def norm_rows(values, gain, shift):
    mean_row = lax.optimization_barrier(jnp.mean(values, axis=-1, keepdims=True))
    centred = values - mean_row
    variance = lax.optimization_barrier(jnp.mean(centred * centred, axis=-1, keepdims=True))
    return centred * lax.rsqrt(variance + EPS) * gain + shift

def matmul(left, right):
    return jnp.dot(left, right, precision=HIGH, preferred_element_type=jnp.float32)

def window_attn(q_win, k_win, v_win, ids_win):
    heads = q_win.reshape(LEN, HEADS, HD).transpose(1, 0, 2)
    scores = low_back(jnp.einsum('hqd,kd->hqk', heads, k_win, precision=HIGH) * HD ** (-0.5))
    places = jnp.arange(LEN)
    visible = (places[None, :] <= places[:, None]) & (ids_win[None, :] == ids_win[:, None])
    scores = jnp.where(visible[None], scores, -1e+30)
    peak = lax.optimization_barrier(jnp.max(scores, axis=-1, keepdims=True))
    expo = jnp.exp(scores - peak)
    probs = expo / lax.optimization_barrier(jnp.sum(expo, axis=-1, keepdims=True))
    mixed = jnp.einsum('hqk,kd->hqd', low(probs), v_win, precision=HIGH)
    return mixed.transpose(1, 0, 2).reshape(LEN, HEADS * HD)

def mapped_window(packed):
    return jax.checkpoint(window_attn)(*packed)

def forward(inputs, ln1_gain, ln1_bias, q_weight, q_bias, kv_weight, v_bias, o_weight, o_bias, ln2_gain, ln2_bias, up_weight, up_bias, down_weight, down_bias, doc_ids):
    first_in = low(norm_rows(inputs, ln1_gain, ln1_bias))
    queries = low(low_back(matmul(first_in, q_weight) + q_bias))
    kv_shift = jnp.concatenate([jnp.zeros((HD,), jnp.float32), v_bias])
    keyvals = low(matmul(first_in, kv_weight) + kv_shift)
    q_all = queries.reshape(WINDOWS, LEN, HEADS * HD)
    k_all = keyvals[:, :HD].reshape(WINDOWS, LEN, HD)
    v_all = keyvals[:, HD:].reshape(WINDOWS, LEN, HD)
    attended = lax.map(mapped_window, (q_all, k_all, v_all, doc_ids))
    context = low(low_back(attended.reshape(TOKENS, HEADS * HD)))
    resid = inputs + low_back(matmul(context, o_weight) + o_bias)
    second_in = low(norm_rows(resid, ln2_gain, ln2_bias))
    upper = low_back(matmul(second_in, up_weight) + up_bias)
    activ = low(jax.nn.gelu(upper, approximate=True))
    return resid + low_back(matmul(activ, down_weight) + down_bias)

def reference(hidden_in, doc_ids, ln1_gain, ln1_bias, q_weight, q_bias, kv_weight, v_bias, o_weight, o_bias, ln2_gain, ln2_bias, up_weight, up_bias, down_weight, down_bias, cotangent):
    floats = [value.astype(jnp.float32) for value in (hidden_in, ln1_gain, ln1_bias, q_weight, q_bias, kv_weight, v_bias, o_weight, o_bias, ln2_gain, ln2_bias, up_weight, up_bias, down_weight, down_bias)]

    def layer_fn(*values):
        return forward(*values, doc_ids)
    result, pull_back = jax.vjp(layer_fn, *floats)
    grads = pull_back(cotangent.astype(jnp.float32))
    return (result.astype(jnp.bfloat16), grads[0], grads[1], grads[2], grads[3], grads[4], grads[5], grads[6], grads[7], grads[8], grads[9], grads[10], grads[11], grads[12], grads[13], grads[14])
```

```python
from functools import partial

import jax
import jax.numpy as jnp
from jax import lax
from jax.sharding import PartitionSpec as P

EPS = 1e-05
F32 = jnp.float32
BF16 = jnp.bfloat16
ROW_CHUNKS = 2
GRAD_CHUNKS = 4


def log2(n):
    bits = n.bit_length() - 1
    assert 1 << bits == n
    return bits


def reverse_bits(value, n):
    bits = log2(n)
    out = 0
    for b in range(bits):
        out = out | (((value >> b) & 1) << (bits - 1 - b))
    return out


def own_first(values, index, n, axis):
    size = values.shape[axis] // n
    return jnp.concatenate(
        [
            lax.dynamic_slice_in_dim(values, (index ^ reverse_bits(p, n)) * size, size, axis)
            for p in range(n)
        ],
        axis=axis,
    )


def in_order(values, index, n, axis):
    size = values.shape[axis] // n
    spot = reverse_bits(index, n)
    return jnp.concatenate(
        [
            lax.dynamic_slice_in_dim(values, (spot ^ reverse_bits(j, n)) * size, size, axis)
            for j in range(n)
        ],
        axis=axis,
    )


def swap(values, axis_name, bit):
    n = lax.axis_size(axis_name)
    return lax.ppermute(values, axis_name, [(i, i ^ bit) for i in range(n)])


def finish_scatter(kept, sent, axis_name):
    n = lax.axis_size(axis_name)
    total = kept + swap(sent, axis_name, 1)
    bit = 2
    while bit < n:
        half = total.shape[0] // 2
        total = total[:half] + swap(total[half:], axis_name, bit)
        bit *= 2
    return total


def scatter_rows(term, rows, parts):
    n = lax.axis_size("tensor")
    outs = []
    for c in range(parts):
        sent = term(n // 2, n, c)
        kept = term(0, n // 2, c)
        outs.append(finish_scatter(kept, sent, "tensor"))
    return outs


def gather_rows(own):
    n = lax.axis_size("tensor")
    blocks = [own]
    bit = n // 2
    while bit:
        blocks = blocks + [swap(b, "tensor", bit) for b in blocks]
        bit //= 2
    return blocks


def sum_all(values, axis_name):
    n = lax.axis_size(axis_name)
    bit = 1
    while bit < n:
        values = values + swap(values, axis_name, bit)
        bit *= 2
    return values


def layer_norm(values, gain, shift):
    mean_row = jnp.mean(values, axis=-1, keepdims=True)
    centred = values - mean_row
    inv_scale = lax.rsqrt(jnp.mean(centred * centred, axis=-1, keepdims=True) + EPS)
    normed = centred * inv_scale
    return (normed * gain + shift, normed, inv_scale)


def norm_back(grad_out, normed, inv_scale, gain):
    scaled = grad_out * gain
    inner = (
        scaled
        - jnp.mean(scaled, axis=-1, keepdims=True)
        - normed * jnp.mean(scaled * normed, axis=-1, keepdims=True)
    )
    return (inner * inv_scale, jnp.sum(grad_out * normed, axis=0), jnp.sum(grad_out, axis=0))


def visible_mask(ids_win, start, finish):
    query_pos = start + jnp.arange(finish - start)
    key_pos = jnp.arange(finish)
    same_doc = ids_win[start:finish][:, None] == ids_win[:finish][None, :]
    return (key_pos[None, :] <= query_pos[:, None]) & same_doc


def attend_window(q_win, k_win, v_win, ids_win):
    length = ids_win.shape[0]
    block = min(512, length)
    factor = q_win.shape[-1] ** (-0.5)
    outs = []
    sums = []
    for start in range(0, length, block):
        finish = start + block
        scores = (
            jnp.einsum("qhd,kd->hqk", q_win[start:finish], k_win[:finish], preferred_element_type=F32)
            * factor
        )
        visible = visible_mask(ids_win, start, finish)
        scores = jnp.where(visible[None], scores, -1e30)
        peak = jnp.max(scores, axis=-1, keepdims=True)
        expo = jnp.exp(scores - peak)
        total = jnp.sum(expo, axis=-1, keepdims=True)
        probs = (expo / total).astype(BF16)
        outs.append(jnp.einsum("hqk,kd->qhd", probs, v_win[:finish], preferred_element_type=F32))
        sums.append((peak + jnp.log(total))[..., 0])
    return (jnp.concatenate(outs, axis=0), jnp.concatenate(sums, axis=1))


def attend_back(q_win, k_win, v_win, ids_win, lse_win, grad_win):
    length = ids_win.shape[0]
    head_dim = k_win.shape[-1]
    block = min(512, length)
    factor = head_dim ** (-0.5)
    grad_q_parts = []
    grad_keys = jnp.zeros((length, head_dim), F32)
    grad_vals = jnp.zeros((length, head_dim), F32)
    for start in range(0, length, block):
        finish = start + block
        q_part = q_win[start:finish]
        grad_part = grad_win[start:finish]
        scores = (
            jnp.einsum("qhd,kd->hqk", q_part, k_win[:finish], preferred_element_type=F32) * factor
        )
        visible = visible_mask(ids_win, start, finish)
        probs = jnp.where(visible[None], jnp.exp(scores - lse_win[:, start:finish, None]), 0.0)
        grad_probs = jnp.einsum("qhd,kd->hqk", grad_part, v_win[:finish], preferred_element_type=F32)
        grad_vals = grad_vals.at[:finish].add(
            jnp.einsum("hqk,qhd->kd", probs.astype(BF16), grad_part, preferred_element_type=F32)
        )
        delta = jnp.sum(probs * grad_probs, axis=-1, keepdims=True)
        grad_scores = (probs * (grad_probs - delta)).astype(BF16)
        grad_q_parts.append(
            jnp.einsum("hqk,kd->qhd", grad_scores, k_win[:finish], preferred_element_type=F32) * factor
        )
        grad_keys = grad_keys.at[:finish].add(
            jnp.einsum("hqk,qhd->kd", grad_scores, q_part, preferred_element_type=F32) * factor
        )
    return (jnp.concatenate(grad_q_parts, axis=0), grad_keys, grad_vals)


def over_tokens(left, right):
    return jnp.einsum("tf,td->fd", left, right, preferred_element_type=F32)


def back_term(grad, weight):
    return jnp.einsum("td,fd->tf", grad, weight, preferred_element_type=F32)


def forward_term(values, weight):
    return jnp.dot(values, weight, preferred_element_type=F32)


def column_sum(values):
    return jnp.sum(values.astype(F32), axis=0)


def two_terms(values):
    high = values.astype(BF16)
    low = (values - high.astype(F32)).astype(BF16)
    return high, low


def on_device(
    hidden_in,
    doc_ids,
    ln1_gain,
    ln1_bias,
    q_weight,
    q_bias,
    kv_weight,
    v_bias,
    o_weight,
    o_bias,
    ln2_gain,
    ln2_bias,
    up_weight,
    up_bias,
    down_weight,
    down_bias,
    cotangent,
):
    n_t = lax.axis_size("tensor")
    n_d = lax.axis_size("dp")
    t = lax.axis_index("tensor")
    d = lax.axis_index("dp")
    rows_here, width = hidden_in.shape
    windows, length = doc_ids.shape
    head_dim = kv_weight.shape[1] // 2
    heads = q_weight.shape[1] // head_dim
    units = up_weight.shape[1]
    own_rows = rows_here // n_t
    part_rows = own_rows // ROW_CHUNKS

    def pick(values, lo, hi, c):
        cols = values.shape[1]
        blocks = values.reshape(n_t, own_rows, cols)[lo:hi, c * part_rows : (c + 1) * part_rows]
        return blocks.reshape((hi - lo) * part_rows, cols)

    def own_part(values, c):
        return values[c * part_rows : (c + 1) * part_rows]

    inputs = hidden_in.astype(F32)
    normed_one, _, _ = layer_norm(inputs, ln1_gain, ln1_bias)
    first_in = normed_one.astype(BF16)
    queries = (forward_term(first_in, q_weight) + q_bias).astype(BF16)
    kv_shift = jnp.concatenate([jnp.zeros((head_dim,), F32), v_bias.astype(F32)])
    keyvals = (forward_term(first_in, kv_weight) + kv_shift).astype(BF16)
    q_all = queries.reshape(windows, length, heads, head_dim)
    k_all = keyvals[:, :head_dim].reshape(windows, length, head_dim)
    v_all = keyvals[:, head_dim:].reshape(windows, length, head_dim)
    attended = [attend_window(q_all[w], k_all[w], v_all[w], doc_ids[w]) for w in range(windows)]
    context = jnp.concatenate([a[0].reshape(length, heads * head_dim) for a in attended], axis=0)
    context = own_first(context.astype(BF16), t, n_t, 0)
    attn_parts = scatter_rows(
        lambda lo, hi, c: forward_term(pick(context, lo, hi, c), o_weight), rows_here, ROW_CHUNKS
    )

    own_in = lax.dynamic_slice_in_dim(hidden_in, t * own_rows, own_rows, 0).astype(F32)
    resid_parts = []
    plain_two_parts = []
    scale_two_parts = []
    gathered = []
    for c in range(ROW_CHUNKS):
        resid = own_part(own_in, c) + attn_parts[c] + o_bias
        _, plain, scale = layer_norm(resid, ln2_gain, ln2_bias)
        resid_parts.append(resid)
        plain_two_parts.append(plain)
        scale_two_parts.append(scale)
        gathered.append(gather_rows(plain))
    plain_all = jnp.concatenate(
        [gathered[c][k] for k in range(n_t) for c in range(ROW_CHUNKS)], axis=0
    )
    second_in = (plain_all * ln2_gain + ln2_bias).astype(BF16)

    grad_out = own_first(cotangent, t, n_t, 0)
    grad_out_cols = own_first(grad_out, d, n_d, 1)
    grad_activ = back_term(grad_out, down_weight)
    upper = forward_term(second_in, up_weight) + up_bias
    activ, gelu_pull = jax.vjp(partial(jax.nn.gelu, approximate=True), upper)
    activ = activ.astype(BF16)
    grad_upper = gelu_pull(grad_activ)[0].astype(BF16)
    up_bias_grad = column_sum(grad_upper)

    def chunked(left, right, chunks):
        half = left.shape[1] // 2
        step = right.shape[1] // chunks
        outs = []
        for c in range(chunks):
            piece = right[:, c * step : (c + 1) * step]
            sent = over_tokens(left[:, half:], piece)
            kept = over_tokens(left[:, :half], piece)
            outs.append(finish_scatter(kept, sent, "dp"))
        return jnp.concatenate(outs, axis=1)

    down_grad = chunked(grad_out_cols, activ, GRAD_CHUNKS).T
    second_grad_parts = scatter_rows(
        lambda lo, hi, c: back_term(pick(grad_upper, lo, hi, c), up_weight), rows_here, ROW_CHUNKS
    )
    up_grad = chunked(own_first(second_in, d, n_d, 1), grad_upper, GRAD_CHUNKS)
    down_parts = scatter_rows(
        lambda lo, hi, c: forward_term(pick(activ, lo, hi, c), down_weight), rows_here, ROW_CHUNKS
    )
    layer_out = jnp.concatenate(
        [resid_parts[c] + down_parts[c] + down_bias for c in range(ROW_CHUNKS)], axis=0
    ).astype(BF16)

    own_cot = lax.dynamic_slice_in_dim(cotangent, t * own_rows, own_rows, 0).astype(F32)
    grad_resid_parts = []
    ln2_gain_grad = 0.0
    ln2_bias_grad = 0.0
    gathered = []
    for c in range(ROW_CHUNKS):
        back, gain_grad, bias_grad = norm_back(
            second_grad_parts[c], plain_two_parts[c], scale_two_parts[c], ln2_gain
        )
        grad_resid = own_part(own_cot, c) + back
        grad_resid_parts.append(grad_resid)
        ln2_gain_grad = ln2_gain_grad + gain_grad
        ln2_bias_grad = ln2_bias_grad + bias_grad
        gathered.append(gather_rows(back))
    grad_resid_own = jnp.concatenate(grad_resid_parts, axis=0)
    back_all = jnp.concatenate(
        [gathered[c][k] for k in range(n_t) for c in range(ROW_CHUNKS)], axis=0
    )
    grad_attn = (grad_out.astype(F32) + back_all).astype(BF16)
    o_bias_grad = column_sum(grad_resid_own.astype(BF16))
    down_bias_grad = column_sum(own_cot)

    grad_context = in_order(back_term(grad_attn, o_weight).astype(BF16), t, n_t, 0)
    o_grad = chunked(own_first(grad_attn, d, n_d, 1), context, 1).T
    grad_ctx_all = grad_context.reshape(windows, length, heads, head_dim)
    pulled = [
        attend_back(q_all[w], k_all[w], v_all[w], doc_ids[w], attended[w][1], grad_ctx_all[w])
        for w in range(windows)
    ]
    grad_query = jnp.concatenate(
        [p[0].reshape(length, heads * head_dim) for p in pulled], axis=0
    ).astype(BF16)
    kv_part = jnp.concatenate(
        [jnp.concatenate([p[1], p[2]], axis=-1) for p in pulled], axis=0
    )
    q_bias_grad = column_sum(grad_query)
    v_bias_grad = jnp.sum(kv_part[:, head_dim:], axis=0)
    kv_high, kv_low = two_terms(kv_part)
    first_cols = own_first(first_in, d, n_d, 1)
    grad_stack = own_first(jnp.concatenate([grad_query, kv_high, kv_low], axis=1), t, n_t, 0)
    weight_stack = jnp.concatenate([q_weight, kv_weight, kv_weight], axis=1)
    first_parts = scatter_rows(
        lambda lo, hi, c: back_term(pick(grad_stack, lo, hi, c), weight_stack), rows_here, ROW_CHUNKS
    )
    q_grad = chunked(first_cols, grad_query, 1)
    kv_cols = own_first(
        first_cols.reshape(rows_here, n_d, n_t, width // (n_d * n_t)), t, n_t, 2
    )
    kv_cols = jnp.swapaxes(kv_cols, 1, 2).reshape(rows_here, width)
    kv_pair = over_tokens(kv_cols, jnp.concatenate([kv_high, kv_low], axis=1))
    kv_term = kv_pair[:, : 2 * head_dim] + kv_pair[:, 2 * head_dim :]
    half = width // 2
    kv_share = finish_scatter(kv_term[:half], kv_term[half:], "tensor")
    half = kv_share.shape[0] // 2
    kv_own = finish_scatter(kv_share[:half], kv_share[half:], "dp")
    kv_grad = in_order(jnp.concatenate(gather_rows(kv_own), axis=0), t, n_t, 0)

    grad_first = jnp.concatenate(first_parts, axis=0)
    _, plain_one, scale_one = layer_norm(own_in, ln1_gain, ln1_bias)
    grad_in_norm, ln1_gain_grad, ln1_bias_grad = norm_back(grad_first, plain_one, scale_one, ln1_gain)
    input_own = grad_resid_own + grad_in_norm
    input_grad = in_order(jnp.concatenate(gather_rows(input_own), axis=0), t, n_t, 0)

    shared = jnp.concatenate(
        [
            ln1_gain_grad,
            ln1_bias_grad,
            o_bias_grad,
            ln2_gain_grad,
            ln2_bias_grad,
            down_bias_grad,
            v_bias_grad,
        ]
    )
    local = jnp.concatenate([q_bias_grad, up_bias_grad])
    vectors = sum_all(jnp.concatenate([sum_all(shared, "tensor"), local]), "dp")
    names = []
    place = 0
    for size in (width,) * 6 + (head_dim, heads * head_dim, units):
        names.append(vectors[place : place + size])
        place += size
    return (
        layer_out,
        input_grad,
        names[0],
        names[1],
        q_grad,
        names[7],
        kv_grad,
        names[6],
        o_grad,
        names[2],
        names[3],
        names[4],
        up_grad,
        names[8],
        down_grad,
        names[5],
    )


def solution(mesh):
    in_specs = (
        P("dp", None),
        P("dp", None),
        P(),
        P(),
        P(None, "tensor"),
        P("tensor"),
        P(),
        P(),
        P("tensor", None),
        P(),
        P(),
        P(),
        P(None, "tensor"),
        P("tensor"),
        P("tensor", None),
        P(),
        P("dp", None),
    )
    out_specs = (
        P(("dp", "tensor"), None),
        P("dp", None),
        P(),
        P(),
        P("dp", "tensor"),
        P("tensor"),
        P("dp", None),
        P(),
        P("tensor", "dp"),
        P(),
        P(),
        P(),
        P("dp", "tensor"),
        P("tensor"),
        P("tensor", "dp"),
        P(),
    )
    return jax.shard_map(
        on_device, mesh=mesh, in_specs=in_specs, out_specs=out_specs, check_vma=False
    )
```

```python
from functools import partial

import jax
import jax.numpy as jnp
from jax import lax
from jax.experimental import pallas as pl
from jax.experimental.pallas import tpu as pltpu
from jax.sharding import PartitionSpec as P

EPS = 1e-05
F32 = jnp.float32
BF16 = jnp.bfloat16
CHUNKS = 4
PARTS = 2
LANES = 128

class Names:
    def __getattr__(self, name):
        return name


class Store(dict):
    __getattr__ = dict.__getitem__
    __setattr__ = dict.__setitem__


S = Names()

ORDER = (
    S.attn, S.ao_s1, S.ao_k0, S.ao_k1, S.ao_s0, S.cot, S.ao_a1, S.dh3, S.dh2, S.ao_a0, S.dh1, S.a1p, S.dh0,
    S.n1, S.n0, S.g1, S.as1, S.g0, S.as0, S.u2, S.up24_s, S.u1, S.dn14z_s, S.up14_s, S.u0, S.u3, S.join,
    S.ff_s1, S.sp_k1, S.sp_s0, S.ff_k1, S.ff_a1, S.ff_k0, S.sp_k0, S.sp_a0, S.dn14z_q, S.up24_q, S.lo1,
    S.sp_s1, S.sp_a1, S.b0, S.dn14z_k, S.up24_k, S.up14_q, S.b1, S.dn14z_f, S.dn04_s, S.up24_f, S.gb0,
    S.up14_k, S.asb0, S.up34_s, S.gb1, S.asb1, S.dn04_q, S.up14_f, S.dn34_s, S.abw, S.dn04_k, S.fp_k0,
    S.up34_q, S.fp_s0, S.up04_s, S.fp_k1, S.fp_a0, S.dn04_f, S.kv_m, S.up34_k, S.kv_x, S.dn34_q, S.l0,
    S.kv_s, S.up34_f, S.ff_s0, S.dn34_k, S.ff_a0, S.up04_q, S.dn34_f, S.gl0, S.lo0, S.dn24_s, S.up04_k,
    S.kv_q, S.out0, S.oo01_s, S.fp_s1, S.fp_a1, S.up04_f, S.kv_k, S.qq02z_s, S.kv_f, S.l1, S.qq02z_q,
    S.dn24_q, S.qq02z_k, S.qq02z_f, S.gl1, S.dn24_k, S.oo01_q, S.out1, S.kv_g0, S.v_0, S.kv_o, S.v_1,
    S.qq12_s, S.dn24_f, S.v_2, S.oo01_k, S.qq12_q, S.oo01_f, S.qq12_k, S.v_3, S.qq12_f, S.v_4, S.v_5,
)


def reverse_bits(value, n):
    bits = n.bit_length() - 1
    assert 1 << bits == n
    out = 0
    for b in range(bits):
        out = out | (((value >> b) & 1) << (bits - 1 - b))
    return out


def quarter_order(n):
    rest = n // 4
    return [low + 4 * reverse_bits(i, rest) for low in (0, 2, 3, 1) for i in range(rest)]


def swap(values, axis_name, bit):
    n = lax.axis_size(axis_name)
    return lax.ppermute(values, axis_name, [(i, i ^ bit) for i in range(n)])


def layer_norm(values):
    mean_row = jnp.mean(values, axis=-1, keepdims=True)
    centred = values - mean_row
    inv_scale = lax.rsqrt(jnp.mean(centred * centred, axis=-1, keepdims=True) + EPS)
    return (centred * inv_scale, inv_scale)


def norm_back(grad_out, normed, inv_scale, gain):
    scaled = grad_out * gain
    inner = (
        scaled
        - jnp.mean(scaled, axis=-1, keepdims=True)
        - normed * jnp.mean(scaled * normed, axis=-1, keepdims=True)
    )
    return (inner * inv_scale, jnp.sum(grad_out * normed, axis=0), jnp.sum(grad_out, axis=0))


def visible_mask(ids_win, start, finish):
    query_pos = start + jnp.arange(finish - start)
    key_pos = jnp.arange(finish)
    same_doc = ids_win[start:finish][:, None] == ids_win[:finish][None, :]
    return (key_pos[None, :] <= query_pos[:, None]) & same_doc


def attend_window(q_win, k_win, v_win, ids_win):
    length = ids_win.shape[0]
    block = min(512, length)
    factor = q_win.shape[-1] ** (-0.5)
    outs = []
    sums = []
    for start in range(0, length, block):
        finish = start + block
        scores = (
            jnp.einsum("qhd,kd->hqk", q_win[start:finish], k_win[:finish], preferred_element_type=F32)
            * factor
        )
        visible = visible_mask(ids_win, start, finish)
        scores = jnp.where(visible[None], scores, -1e30)
        peak = jnp.max(scores, axis=-1, keepdims=True)
        expo = jnp.exp(scores - peak)
        total = jnp.sum(expo, axis=-1, keepdims=True)
        probs = (expo / total).astype(BF16)
        outs.append(jnp.einsum("hqk,kd->qhd", probs, v_win[:finish], preferred_element_type=F32))
        sums.append((peak + jnp.log(total))[..., 0])
    return (jnp.concatenate(outs, axis=0), jnp.concatenate(sums, axis=1))


def attend_back(q_win, k_win, v_win, ids_win, lse_win, grad_win):
    length = ids_win.shape[0]
    head_dim = k_win.shape[-1]
    block = min(512, length)
    factor = head_dim ** (-0.5)
    grad_q_parts = []
    grad_keys = jnp.zeros((length, head_dim), F32)
    grad_vals = jnp.zeros((length, head_dim), F32)
    for start in range(0, length, block):
        finish = start + block
        q_part = q_win[start:finish]
        grad_part = grad_win[start:finish]
        scores = (
            jnp.einsum("qhd,kd->hqk", q_part, k_win[:finish], preferred_element_type=F32) * factor
        )
        visible = visible_mask(ids_win, start, finish)
        probs = jnp.where(visible[None], jnp.exp(scores - lse_win[:, start:finish, None]), 0.0)
        grad_probs = jnp.einsum("qhd,kd->hqk", grad_part, v_win[:finish], preferred_element_type=F32)
        grad_vals = grad_vals.at[:finish].add(
            jnp.einsum("hqk,qhd->kd", probs.astype(BF16), grad_part, preferred_element_type=F32)
        )
        delta = jnp.sum(probs * grad_probs, axis=-1, keepdims=True)
        grad_scores = (probs * (grad_probs - delta)).astype(BF16)
        grad_q_parts.append(
            jnp.einsum("hqk,kd->qhd", grad_scores, k_win[:finish], preferred_element_type=F32) * factor
        )
        grad_keys = grad_keys.at[:finish].add(
            jnp.einsum("hqk,qhd->kd", grad_scores, q_part, preferred_element_type=F32) * factor
        )
    return (jnp.concatenate(grad_q_parts, axis=0), grad_keys, grad_vals)


def over_tokens(left, right):
    return jnp.einsum("tf,td->fd", left, right, preferred_element_type=F32)


def back_term(grad, weight):
    return jnp.einsum("td,fd->tf", grad, weight, preferred_element_type=F32)


def forward_term(values, weight):
    return jnp.dot(values, weight, preferred_element_type=F32)


def column_sum(values):
    return jnp.sum(values.astype(F32), axis=0)


def mix_columns(values, spots, n):
    size = values.shape[1] // n
    return jnp.take(values, (spots[:, None] * size + jnp.arange(size)[None, :]).reshape(-1), axis=1)


def arrange(values, row_spots, col_spots, plain, mixed):
    n_rows, n_cols = row_spots.shape[0], col_spots.shape[0]
    height, width = values.shape[0] // n_rows, values.shape[1]
    size = width // n_cols
    if mixed and size % LANES:
        both = arrange(values, row_spots, col_spots, True, False)
        mix = (mix_columns(both[0], col_spots, n_cols),)
        return both + mix if plain else mix
    fan = n_rows // 2 if width * height * n_rows > (1 << 20) else n_rows

    def body(rows, cols, *refs):
        ins, outs = refs[:fan], list(refs[fan:])
        if plain:
            out = outs.pop(0)
            for k in range(fan):
                out[k * height : (k + 1) * height, :] = ins[k][...]
        if mixed:
            out = outs.pop(0)
            for k in range(fan):
                for p in range(n_cols):
                    place = pl.multiple_of(cols[p] * size, LANES)
                    out[k * height : (k + 1) * height, p * size : (p + 1) * size] = ins[k][:, pl.ds(place, size)]

    count = int(plain) + int(mixed)
    out = pl.pallas_call(
        body,
        out_shape=[jax.ShapeDtypeStruct(values.shape, values.dtype)] * count,
        grid_spec=pltpu.PrefetchScalarGridSpec(
            num_scalar_prefetch=2,
            grid=(n_rows // fan,),
            in_specs=[
                pl.BlockSpec((height, width), lambda i, rows, cols, k=k: (rows[i * fan + k], 0))
                for k in range(fan)
            ],
            out_specs=[pl.BlockSpec((fan * height, width), lambda i, rows, cols: (i, 0))] * count,
        ),
        name="arrange",
    )(row_spots, col_spots, *([values] * fan))
    return tuple(out)


def take_in(pieces, shared, part, col_spots, combine, earlier):
    count = len(pieces)
    height, width = pieces[0].shape
    n_cols = col_spots.shape[0]
    size = width // n_cols
    mixing = size % LANES == 0
    outputs = 2 if mixing else 1
    strip = height // 4

    def body(cols, *refs):
        ins, rest = refs[:count], refs[count:]
        extra = rest[: len(shared)]
        outs = rest[len(rest) - outputs :]
        for p in range(count):
            block = [e[0, p] if len(e.shape) == 4 else e[...] for e in extra]
            outs[0][0, p] = combine(ins[p][...], *block).astype(BF16)
            if mixing:
                for k in range(n_cols):
                    place = pl.multiple_of(cols[k] * size, LANES)
                    outs[1][0, p, :, k * size : (k + 1) * size] = outs[0][0, p, :, pl.ds(place, size)]

    rows_block = pl.BlockSpec((1, count, strip, width), lambda i, cols: (part, 0, i, 0))
    in_specs = [pl.BlockSpec((strip, width), lambda i, cols: (i, 0))] * count
    operands = list(pieces)
    for s in shared:
        if s.shape[0] == 1:
            in_specs.append(pl.BlockSpec((1, width), lambda i, cols: (0, 0)))
            operands.append(s)
        else:
            in_specs.append(rows_block)
            operands.append(s.reshape(PARTS, count, height, width))
    aliases = {}
    if earlier is not None:
        for k in range(outputs):
            aliases[1 + len(operands)] = k
            operands.append(earlier[k].reshape(PARTS, count, height, width))
            in_specs.append(pl.BlockSpec(memory_space=pl.ANY))
    out = pl.pallas_call(
        body,
        out_shape=[jax.ShapeDtypeStruct((PARTS, count, height, width), BF16)] * outputs,
        grid_spec=pltpu.PrefetchScalarGridSpec(
            num_scalar_prefetch=1,
            grid=(height // strip,),
            in_specs=in_specs,
            out_specs=[rows_block] * outputs,
        ),
        input_output_aliases=aliases,
        name="take_in",
    )(col_spots, *operands)
    return tuple(o.reshape(PARTS * count * height, width) for o in out)


def place_rows(pieces, row_spots, total_rows, earlier):
    count = len(pieces)
    height, width = pieces[0].shape

    def body(rows, *refs):
        i = pl.program_id(0)
        for p in range(count):

            @pl.when(i == p)
            def _():
                refs[-1][...] = refs[p][...]

    operands = list(pieces)
    in_specs = [pl.BlockSpec((height, width), lambda i, rows: (0, 0))] * count
    aliases = {}
    if earlier is not None:
        aliases[1 + count] = 0
        operands.append(earlier)
        in_specs.append(pl.BlockSpec(memory_space=pl.ANY))
    return pl.pallas_call(
        body,
        out_shape=jax.ShapeDtypeStruct((total_rows, width), F32),
        grid_spec=pltpu.PrefetchScalarGridSpec(
            num_scalar_prefetch=1,
            grid=(count,),
            in_specs=in_specs,
            out_specs=pl.BlockSpec((height, width), lambda i, rows: (rows[i], 0)),
        ),
        input_output_aliases=aliases,
        name="place_rows",
    )(row_spots, *operands)


def on_device(
    hidden_in,
    doc_ids,
    ln1_gain,
    ln1_bias,
    q_weight,
    q_bias,
    kv_weight,
    v_bias,
    o_weight,
    o_bias,
    ln2_gain,
    ln2_bias,
    up_weight,
    up_bias,
    down_weight,
    down_bias,
    cotangent,
):
    n_t = lax.axis_size("tensor")
    n_d = lax.axis_size("dp")
    assert n_t == 4 and n_d >= 4
    t = lax.axis_index("tensor")
    d = lax.axis_index("dp")
    rows_here, width = hidden_in.shape
    windows, length = doc_ids.shape
    head_dim = kv_weight.shape[1] // 2
    heads = q_weight.shape[1] // head_dim
    units = up_weight.shape[1]
    own_rows = rows_here // n_t
    piece = own_rows // PARTS
    part_rows = rows_here // PARTS

    t_order = [reverse_bits(p, n_t) for p in range(n_t)]
    part_spots = [jnp.stack([(t ^ k) * PARTS + c for k in t_order]).astype(jnp.int32) for c in range(PARTS)]
    row_spots = jnp.concatenate(part_spots)
    row_back = jnp.stack(
        [c * n_t + reverse_bits(t ^ j, n_t) for j in range(n_t) for c in range(PARTS)]
    ).astype(jnp.int32)
    row_same = jnp.arange(n_t * PARTS, dtype=jnp.int32)
    col_spots = jnp.stack([d ^ k for k in quarter_order(n_d)]).astype(jnp.int32)

    state = Store()
    steps = {}
    last = []

    def define(name):
        def put(fn):
            steps[name.replace(".", "_")] = fn
            return fn

        return put

    def hold(*values):
        if not last:
            return values if len(values) > 1 else values[0]
        out = lax.optimization_barrier(tuple(values) + (last[-1],))
        return out[:-1] if len(values) > 1 else out[0]

    def done(value):
        last[:] = [value]

    def part_of(values, c):
        return values[c * part_rows : (c + 1) * part_rows]

    @define(S.attn)
    def _():
        normed, _ = layer_norm(hidden_in.astype(F32))
        first_in = (normed * ln1_gain + ln1_bias).astype(BF16)
        queries = (forward_term(first_in, q_weight) + q_bias).astype(BF16)
        kv_shift = jnp.concatenate([jnp.zeros((head_dim,), F32), v_bias.astype(F32)])
        keyvals = (forward_term(first_in, kv_weight) + kv_shift).astype(BF16)
        q_all = queries.reshape(windows, length, heads, head_dim)
        k_all = keyvals[:, :head_dim].reshape(windows, length, head_dim)
        v_all = keyvals[:, head_dim:].reshape(windows, length, head_dim)
        attended = [attend_window(q_all[w], k_all[w], v_all[w], doc_ids[w]) for w in range(windows)]
        context = jnp.concatenate([a[0].reshape(length, heads * head_dim) for a in attended], axis=0)
        context = arrange(context.astype(BF16), row_spots, col_spots, True, False)[0]
        state.update(first_in=first_in, q=q_all, k=k_all, v=v_all, lse=[a[1] for a in attended])
        state.update(context=context)
        done(context)

    @define(S.cot)
    def _():
        state.cot, state.cot_cols = arrange(hold(cotangent), row_spots, col_spots, True, True)
        done(state.cot_cols)

    unit_step = units // CHUNKS

    for k in range(CHUNKS):
        here = slice(k * unit_step, (k + 1) * unit_step)

        @define(f"dh{k}")
        def _(k=k, here=here):
            state[f"dh{k}"] = back_term(hold(state.cot), down_weight[here])
            done(state[f"dh{k}"])

        @define(f"u{k}")
        def _(k=k, here=here):
            second = hold(state.second_pair[0])
            upper = forward_term(second, up_weight[:, here]) + up_bias[here]
            value, pull = jax.vjp(partial(jax.nn.gelu, approximate=True), upper)
            state[f"h{k}"] = value.astype(BF16)
            state[f"du{k}"] = pull(state[f"dh{k}"])[0].astype(BF16)
            done(state[f"h{k}"])

    @define(S.join)
    def _():
        parts = hold(*[state[f"{name}{k}"] for name in ("h", "du") for k in range(CHUNKS)])
        state.activ = jnp.concatenate(parts[:CHUNKS], axis=1)
        state.grad_upper = jnp.concatenate(parts[CHUNKS:], axis=1)
        state.up_sum = column_sum(state.grad_upper)
        done(state.grad_upper)

    @define(S.a1p)
    def _():
        state.first_cols = arrange(hold(state.first_in), row_same, col_spots, False, True)[0]
        done(state.first_cols)

    def row_sum(tag, values, multiply, c):
        low = c * part_rows
        middle = low + part_rows // 2

        @define(f"{tag}_s{c}")
        def _():
            sent = multiply(hold(values()[middle : middle + part_rows // 2]))
            state[f"{tag}_c{c}"] = swap(sent, "tensor", 1)
            done(sent)

        @define(f"{tag}_k{c}")
        def _():
            total = multiply(hold(values()[low:middle]))
            state[f"{tag}_kept{c}"] = total
            done(total)

        @define(f"{tag}_a{c}")
        def _():
            arrived = hold(state[f"{tag}_c{c}"])
            kept = state[f"{tag}_kept{c}"]
            sent = kept[piece:] + arrived[piece:]
            state[f"{tag}_near{c}"] = arrived
            state[f"{tag}_x{c}"] = swap(sent, "tensor", 2)
            done(sent)

    def own_sum(tag, c):
        arrived = hold(state[f"{tag}_x{c}"])
        return state[f"{tag}_kept{c}"][:piece] + state[f"{tag}_near{c}"][:piece] + arrived

    def spread(tag, values, c):
        state[f"{tag}{c}"] = values
        state[f"{tag}x{c}"] = swap(values, "tensor", 2)

    def pass_on(name, tag, c):
        @define(f"{name}{c}")
        def _():
            arrived = hold(state[f"{tag}x{c}"])
            state[f"{tag}x{c}"] = arrived
            state[f"{tag}c{c}"] = swap(state[f"{tag}{c}"], "tensor", 1)
            state[f"{tag}g{c}"] = swap(arrived, "tensor", 1)
            done(arrived)

    def pieces_of(tag, c):
        return hold(state[f"{tag}{c}"], state[f"{tag}x{c}"], state[f"{tag}c{c}"], state[f"{tag}g{c}"])

    own_in = lax.dynamic_slice_in_dim(hidden_in, t * own_rows, own_rows, 0)
    own_cot = lax.dynamic_slice_in_dim(cotangent, t * own_rows, own_rows, 0)

    def own_part(values, c):
        return values[c * piece : (c + 1) * piece].astype(F32)

    for c in range(PARTS):
        row_sum("ao", lambda: state.context, lambda v: forward_term(v, o_weight), c)

        @define(f"n{c}")
        def _(c=c):
            resid = own_part(own_in, c) + own_sum("ao", c) + o_bias
            plain, scale = layer_norm(resid)
            state[f"resid{c}"] = resid
            state[f"scale{c}"] = scale
            spread("n", plain, c)
            done(plain)

        pass_on("g", "n", c)

        @define(f"as{c}")
        def _(c=c):
            out = take_in(
                pieces_of("n", c),
                [ln2_gain.reshape(1, width), ln2_bias.reshape(1, width)],
                c,
                col_spots,
                lambda v, g, b: v * g.astype(F32) + b.astype(F32),
                state.get(S.second_pair),
            )
            state.second_pair = out
            done(out[0])

        row_sum("sp", lambda: state.grad_upper, lambda v: back_term(v, up_weight), c)
        row_sum("ff", lambda: state.activ, lambda v: forward_term(v, down_weight), c)

        @define(f"lo{c}")
        def _(c=c):
            state[f"out{c}"] = (state[f"resid{c}"] + own_sum("ff", c) + down_bias).astype(BF16)
            done(state[f"out{c}"])

        @define(f"b{c}")
        def _(c=c):
            grad_second = own_sum("sp", c)
            back, gain_grad, bias_grad = norm_back(
                grad_second, state[f"n{c}"], state[f"scale{c}"], ln2_gain
            )
            spread("b", back, c)
            state[f"grad_resid{c}"] = own_part(own_cot, c) + back
            state[f"ln2_{c}"] = (gain_grad, bias_grad)
            done(back)

        pass_on("gb", "b", c)

        @define(f"asb{c}")
        def _(c=c):
            out = take_in(
                pieces_of("b", c),
                [state.cot],
                c,
                col_spots,
                lambda v, g: g.astype(F32) + v,
                state.get(S.attn_pair),
            )
            state.attn_pair = out
            done(out[0])

        row_sum("fp", lambda: state.stack, lambda v: back_term(v, state.stack_w), c)

        @define(f"l{c}")
        def _(c=c):
            grad_first = own_sum("fp", c)
            plain, scale = layer_norm(own_part(own_in, c))
            back, gain_grad, bias_grad = norm_back(grad_first, plain, scale, ln1_gain)
            result = state[f"grad_resid{c}"] + back
            spread("l", result, c)
            state[f"ln1_{c}"] = (gain_grad, bias_grad)
            done(result)

        pass_on("gl", "l", c)

        @define(f"out{c}")
        def _(c=c):
            out = place_rows(pieces_of("l", c), part_spots[c], rows_here, state.get(S.input_grad))
            state.input_grad = out
            done(out)

    @define(S.abw)
    def _():
        grad_attn = hold(state.attn_pair[0])
        grad_context = back_term(grad_attn, o_weight).astype(BF16)
        grad_context = arrange(grad_context, row_back, col_spots, True, False)[0]
        grad_ctx_all = grad_context.reshape(windows, length, heads, head_dim)
        pulled = [
            attend_back(state.q[w], state.k[w], state.v[w], doc_ids[w], state.lse[w], grad_ctx_all[w])
            for w in range(windows)
        ]
        grad_query = jnp.concatenate(
            [p[0].reshape(length, heads * head_dim) for p in pulled], axis=0
        ).astype(BF16)
        kv_part = jnp.concatenate([jnp.concatenate([p[1], p[2]], axis=-1) for p in pulled], axis=0)
        high = kv_part.astype(BF16)
        low = (kv_part - high.astype(F32)).astype(BF16)
        stack = jnp.concatenate([grad_query, high, low], axis=1)
        state.grad_query = grad_query
        state.kv_terms = jnp.concatenate([high, low], axis=1)
        state.q_sum = column_sum(grad_query)
        state.v_sum = jnp.sum(kv_part[:, head_dim:], axis=0)
        state.stack = arrange(stack, row_spots, col_spots, True, False)[0]
        state.stack_w = jnp.concatenate([q_weight, kv_weight, kv_weight], axis=1)
        done(state.stack)

    half = width // 2
    quarter = width // 4

    def cut(values, lo, hi, axis):
        return lax.slice_in_dim(values, lo, hi, axis=axis)

    def tail(values, axis):
        middle = values.shape[axis] // 2
        return cut(values, 0, middle, axis), cut(values, middle, 2 * middle, axis)

    def finish(kept, sent_back, axis, bit):
        total = kept + sent_back
        while bit < n_d:
            kept, sent = tail(total, axis)
            total = kept + swap(sent, "dp", bit)
            bit *= 2
        return total

    def dims(axis, block, other):
        return (block, other) if axis == 0 else (other, block)

    def grad_low_first(tag, term, axis):
        @define(f"{tag}.s")
        def _():
            sent = term(half, width, hold)
            state[f"{tag}.y"] = swap(sent, "dp", 1)
            done(sent)

        @define(f"{tag}.q")
        def _():
            arrived = hold(state[f"{tag}.y"])
            total = term(quarter, half, lambda v: v) + cut(arrived, 0, quarter, axis)
            state[f"{tag}.rest"] = cut(arrived, quarter, half, axis)
            state[f"{tag}.z1"] = swap(total, "dp", 2)
            done(total)

        @define(f"{tag}.k")
        def _():
            arrived, rest = hold(state[f"{tag}.z1"], state[f"{tag}.rest"])
            total = term(0, quarter, lambda v: v) + rest + arrived
            kept, sent = tail(total, axis)
            state[f"{tag}.kept"] = kept
            state[f"{tag}.z2"] = swap(sent, "dp", 4)
            done(total)

        @define(f"{tag}.f")
        def _():
            arrived = hold(state[f"{tag}.z2"])
            state[tag] = finish(state[f"{tag}.kept"], arrived, axis, 8)
            done(state[tag])

    def grad_high_first(tag, term, axis):
        @define(f"{tag}.s")
        def _():
            sent = term(quarter, 3 * quarter, hold)
            state[f"{tag}.z1"] = swap(sent, "dp", 2)
            done(sent)

        @define(f"{tag}.q")
        def _():
            arrived = hold(state[f"{tag}.z1"])
            near = term(0, quarter, lambda v: v) + cut(arrived, 0, quarter, axis)
            far = term(3 * quarter, width, lambda v: v) + cut(arrived, quarter, half, axis)
            near, near_sent = tail(near, axis)
            far, far_sent = tail(far, axis)
            sent = jnp.concatenate([near_sent, far_sent], axis=axis)
            state[f"{tag}.kept"] = (near, far)
            state[f"{tag}.z2"] = swap(sent, "dp", 4)
            done(sent)

        @define(f"{tag}.k")
        def _():
            arrived = hold(state[f"{tag}.z2"])
            near, far = state[f"{tag}.kept"]
            a, b = tail(arrived, axis)
            near = finish(near, a, axis, 8)
            far = finish(far, b, axis, 8)
            state[f"{tag}.kept"] = near
            state[f"{tag}.y"] = swap(far, "dp", 1)
            done(far)

        @define(f"{tag}.f")
        def _():
            arrived = hold(state[f"{tag}.y"])
            state[tag] = state[f"{tag}.kept"] + arrived
            done(state[tag])

    def mixed_of(pair_name):
        pair = state[pair_name]
        return pair[1] if len(pair) > 1 else mix_columns(pair[0], col_spots, n_d)

    def rows_term(left, right):
        def term(lo, hi, h):
            return over_tokens(h(left()[:, lo:hi]), right())

        return term

    def cols_term(left, right):
        def term(lo, hi, h):
            return over_tokens(left(), h(right()[:, lo:hi]))

        return term

    def piece_of(get, k, n):
        def f():
            values = get()
            size = values.shape[1] // n
            return values[:, k * size : (k + 1) * size]

        return f

    for name in ORDER:
        if not name.endswith("_s") or name.startswith("kv"):
            continue
        tag = name[:-2]
        kind, index = tag[:2], tag[2:]
        k, n, high = int(index[0]), int(index[1]), index.endswith("z")
        make = grad_high_first if high else grad_low_first
        if kind == "dn":
            make(tag, cols_term(lambda k=k: state[f"h{k}"], lambda: state.cot_cols), 1)
        elif kind == "up":
            make(tag, rows_term(lambda: mixed_of("second_pair"), lambda k=k: state[f"du{k}"]), 0)
        elif kind == "oo":
            make(tag, cols_term(piece_of(lambda: state.context, k, n), lambda: mixed_of("attn_pair")), 1)
        else:
            make(tag, rows_term(lambda: state.first_cols, piece_of(lambda: state.grad_query, k, n)), 0)

    def joined(kind, axis):
        found = sorted(name[:-2] for name in ORDER if name.startswith(kind) and name.endswith("_s"))
        return jnp.concatenate([state[tag] for tag in found], axis=axis)

    share = width // (n_d * n_t)

    @define(S.kv_m)
    def _():
        pair = over_tokens(hold(state.first_cols), state.kv_terms)
        term = (pair[:, : 2 * head_dim] + pair[:, 2 * head_dim :]).reshape(n_d, 2, 2, share, 2 * head_dim)
        core = t & 1
        sent = lax.dynamic_index_in_dim(term, 1 - core, 2, keepdims=False)
        state.kv_keep = lax.dynamic_index_in_dim(term, core, 2, keepdims=False)
        state.kv_c = swap(sent, "tensor", 1)
        done(sent)

    @define(S.kv_x)
    def _():
        total = state.kv_keep + hold(state.kv_c)
        chip = t >> 1
        sent = lax.dynamic_index_in_dim(total, 1 - chip, 1, keepdims=False)
        state.kv_keep = lax.dynamic_index_in_dim(total, chip, 1, keepdims=False)
        state.kv_xx = swap(sent, "tensor", 2)
        done(sent)

    @define(S.kv_s)
    def _():
        total = (state.kv_keep + hold(state.kv_xx)).reshape(n_d * share, 2 * head_dim)
        quart = n_d * share // 4
        state.kv_q1, state.kv_q0 = total[quart : 2 * quart], total[:quart]
        sent = total[2 * quart :]
        state.kv_y = swap(sent, "dp", 1)
        done(sent)

    @define(S.kv_q)
    def _():
        arrived = hold(state.kv_y)
        quart = n_d * share // 4
        sent = state.kv_q1 + arrived[:quart]
        state.kv_q0 = state.kv_q0 + arrived[quart:]
        state.kv_z1 = swap(sent, "dp", 2)
        done(sent)

    @define(S.kv_k)
    def _():
        total = state.kv_q0 + hold(state.kv_z1)
        kept, sent = tail(total, 0)
        state.kv_keep = kept
        state.kv_z2 = swap(sent, "dp", 4)
        done(total)

    @define(S.kv_f)
    def _():
        total = finish(state.kv_keep, hold(state.kv_z2), 0, 8)
        spread("kv", total, 0)
        done(total)

    pass_on("kv.g", "kv", 0)

    @define(S.kv_o)
    def _():
        own, other_x, other_c, other_cx = pieces_of("kv", 0)
        core, chip = t & 1, t >> 1
        pair = jnp.where(core == 0, jnp.stack([own, other_c]), jnp.stack([other_c, own]))
        pair_x = jnp.where(core == 0, jnp.stack([other_x, other_cx]), jnp.stack([other_cx, other_x]))
        whole = jnp.where(chip == 0, jnp.stack([pair, pair_x]), jnp.stack([pair_x, pair]))
        state.kv_grad = whole.reshape(n_t * share, 2 * head_dim)
        done(state.kv_grad)

    @define(S.v_0)
    def _():
        resid = jnp.concatenate([state[f"grad_resid{c}"] for c in range(PARTS)], axis=0)
        values = jnp.concatenate(
            [
                state.ln1_0[0] + state.ln1_1[0],
                state.ln1_0[1] + state.ln1_1[1],
                column_sum(resid.astype(BF16)),
                state.ln2_0[0] + state.ln2_1[0],
                state.ln2_0[1] + state.ln2_1[1],
                column_sum(own_cot),
                state.v_sum,
            ]
        )
        values = hold(values)
        state.v = values
        state.v_c = swap(values, "tensor", 1)
        done(values)

    @define(S.v_1)
    def _():
        state.v = state.v + hold(state.v_c)
        state.v_x = swap(state.v, "tensor", 2)
        done(state.v)

    @define(S.v_2)
    def _():
        total = state.v + hold(state.v_x)
        up_sum = state.up_sum
        state.v = jnp.concatenate([total, state.q_sum, up_sum])
        state.v_y = swap(state.v, "dp", 1)
        done(state.v)

    @define(S.v_3)
    def _():
        state.v = state.v + hold(state.v_y)
        state.v_z1 = swap(state.v, "dp", 2)
        done(state.v)

    @define(S.v_4)
    def _():
        state.v = state.v + hold(state.v_z1)
        state.v_z2 = swap(state.v, "dp", 4)
        done(state.v)

    @define(S.v_5)
    def _():
        total = state.v + hold(state.v_z2)
        bit = 8
        while bit < n_d:
            total = total + swap(total, "dp", bit)
            bit *= 2
        state.v = total
        done(total)

    for name in ORDER:
        with jax.named_scope("step." + name):
            steps[name]()

    vectors = []
    place = 0
    for size in (width,) * 6 + (head_dim, heads * head_dim, units):
        vectors.append(state.v[place : place + size])
        place += size
    return (
        jnp.concatenate([state.out0, state.out1], axis=0),
        state.input_grad,
        vectors[0],
        vectors[1],
        joined("qq", 1),
        vectors[7],
        state.kv_grad,
        vectors[6],
        joined("oo", 0),
        vectors[2],
        vectors[3],
        vectors[4],
        joined("up", 1),
        vectors[8],
        joined("dn", 0),
        vectors[5],
    )


def solution(mesh):
    in_specs = (
        P("dp", None),
        P("dp", None),
        P(),
        P(),
        P(None, "tensor"),
        P("tensor"),
        P(),
        P(),
        P("tensor", None),
        P(),
        P(),
        P(),
        P(None, "tensor"),
        P("tensor"),
        P("tensor", None),
        P(),
        P("dp", None),
    )
    out_specs = (
        P(("dp", "tensor"), None),
        P("dp", None),
        P(),
        P(),
        P("dp", "tensor"),
        P("tensor"),
        P("dp", None),
        P(),
        P("tensor", "dp"),
        P(),
        P(),
        P(),
        P("dp", "tensor"),
        P("tensor"),
        P("tensor", "dp"),
        P(),
    )
    return jax.shard_map(
        on_device, mesh=mesh, in_specs=in_specs, out_specs=out_specs, check_vma=False
    )
```

```python
from functools import partial

import jax
import jax.numpy as jnp
from jax import lax
from jax.experimental import pallas as pl
from jax.experimental.pallas import tpu as pltpu
from jax.sharding import PartitionSpec as P

EPS = 1e-05
F32 = jnp.float32
BF16 = jnp.bfloat16
CHUNKS = 4
PARTS = 2
LANES = 128

class Names:
    def __getattr__(self, name):
        return name


class Store(dict):
    __getattr__ = dict.__getitem__
    __setattr__ = dict.__setitem__


S = Names()

ORDER = (
    S.attn, S.ao_s1, S.ao_k0, S.ao_k1, S.cot, S.ao_s0, S.ao_a1, S.dh2, S.a1p, S.dh3, S.ao_a0, S.dh0, S.n1,
    S.dh1, S.n0, S.g1, S.g0, S.as1, S.as0, S.u1, S.dn14z_s, S.up14_s, S.u0, S.dn04_s, S.u3, S.u2, S.join,
    S.sp_s0, S.ff_k1, S.dn14z_q, S.ff_s1, S.ff_k0, S.up14_q, S.sp_k1, S.ff_a1, S.sp_k0, S.sp_a0, S.dn14z_k,
    S.up14_k, S.dn04_q, S.dn14z_f, S.dn34_s, S.lo1, S.sp_s1, S.b0, S.up14_f, S.up04_s, S.dn04_k, S.sp_a1,
    S.dn34_q, S.dn04_f, S.gb0, S.b1, S.dn34_k, S.asb0, S.up24_s, S.gb1, S.up04_q, S.dn34_f, S.up34_s,
    S.asb1, S.up04_k, S.abw, S.up24_q, S.oo01_s, S.fp_s0, S.fp_k1, S.fp_k0, S.up04_f, S.ff_s0, S.fp_a0,
    S.up24_k, S.up34_q, S.ff_a0, S.l0, S.up24_f, S.qq12_s, S.up34_k, S.oo01_q, S.lo0, S.dn24_s, S.up34_f,
    S.gl0, S.oo01_k, S.qq12_q, S.out0, S.kv_m, S.fp_s1, S.oo01_f, S.qq12_k, S.dn24_q, S.kv_x, S.fp_a1,
    S.qq12_f, S.kv_s, S.dn24_k, S.kv_q, S.l1, S.v_0, S.dn24_f, S.kv_k, S.qq02z_s, S.v_1, S.gl1, S.kv_f,
    S.v_2, S.qq02z_q, S.v_3, S.out1, S.kv_g0, S.qq02z_k, S.v_4, S.kv_o, S.v_5, S.qq02z_f,
)


def reverse_bits(value, n):
    bits = n.bit_length() - 1
    assert 1 << bits == n
    out = 0
    for b in range(bits):
        out = out | (((value >> b) & 1) << (bits - 1 - b))
    return out


def quarter_order(n):
    rest = n // 4
    return [low + 4 * reverse_bits(i, rest) for low in (0, 2, 3, 1) for i in range(rest)]


def swap(values, axis_name, bit):
    n = lax.axis_size(axis_name)
    return lax.ppermute(values, axis_name, [(i, i ^ bit) for i in range(n)])


def layer_norm(values):
    mean_row = jnp.mean(values, axis=-1, keepdims=True)
    centred = values - mean_row
    inv_scale = lax.rsqrt(jnp.mean(centred * centred, axis=-1, keepdims=True) + EPS)
    return (centred * inv_scale, inv_scale)


def norm_back(grad_out, normed, inv_scale, gain):
    scaled = grad_out * gain
    inner = (
        scaled
        - jnp.mean(scaled, axis=-1, keepdims=True)
        - normed * jnp.mean(scaled * normed, axis=-1, keepdims=True)
    )
    return (inner * inv_scale, jnp.sum(grad_out * normed, axis=0), jnp.sum(grad_out, axis=0))


def visible_mask(ids_win, start, finish):
    query_pos = start + jnp.arange(finish - start)
    key_pos = jnp.arange(finish)
    same_doc = ids_win[start:finish][:, None] == ids_win[:finish][None, :]
    return (key_pos[None, :] <= query_pos[:, None]) & same_doc


def attend_window(q_win, k_win, v_win, ids_win):
    length = ids_win.shape[0]
    block = min(512, length)
    factor = q_win.shape[-1] ** (-0.5)
    outs = []
    sums = []
    for start in range(0, length, block):
        finish = start + block
        scores = (
            jnp.einsum("qhd,kd->hqk", q_win[start:finish], k_win[:finish], preferred_element_type=F32)
            * factor
        )
        visible = visible_mask(ids_win, start, finish)
        scores = jnp.where(visible[None], scores, -1e30)
        peak = jnp.max(scores, axis=-1, keepdims=True)
        expo = jnp.exp(scores - peak)
        total = jnp.sum(expo, axis=-1, keepdims=True)
        probs = (expo / total).astype(BF16)
        outs.append(jnp.einsum("hqk,kd->qhd", probs, v_win[:finish], preferred_element_type=F32))
        sums.append((peak + jnp.log(total))[..., 0])
    return (jnp.concatenate(outs, axis=0), jnp.concatenate(sums, axis=1))


def attend_back(q_win, k_win, v_win, ids_win, lse_win, grad_win):
    length = ids_win.shape[0]
    head_dim = k_win.shape[-1]
    block = min(512, length)
    factor = head_dim ** (-0.5)
    grad_q_parts = []
    grad_keys = jnp.zeros((length, head_dim), F32)
    grad_vals = jnp.zeros((length, head_dim), F32)
    for start in range(0, length, block):
        finish = start + block
        q_part = q_win[start:finish]
        grad_part = grad_win[start:finish]
        scores = (
            jnp.einsum("qhd,kd->hqk", q_part, k_win[:finish], preferred_element_type=F32) * factor
        )
        visible = visible_mask(ids_win, start, finish)
        probs = jnp.where(visible[None], jnp.exp(scores - lse_win[:, start:finish, None]), 0.0)
        grad_probs = jnp.einsum("qhd,kd->hqk", grad_part, v_win[:finish], preferred_element_type=F32)
        grad_vals = grad_vals.at[:finish].add(
            jnp.einsum("hqk,qhd->kd", probs.astype(BF16), grad_part, preferred_element_type=F32)
        )
        delta = jnp.sum(probs * grad_probs, axis=-1, keepdims=True)
        grad_scores = (probs * (grad_probs - delta)).astype(BF16)
        grad_q_parts.append(
            jnp.einsum("hqk,kd->qhd", grad_scores, k_win[:finish], preferred_element_type=F32) * factor
        )
        grad_keys = grad_keys.at[:finish].add(
            jnp.einsum("hqk,qhd->kd", grad_scores, q_part, preferred_element_type=F32) * factor
        )
    return (jnp.concatenate(grad_q_parts, axis=0), grad_keys, grad_vals)


def over_tokens(left, right):
    return jnp.einsum("tf,td->fd", left, right, preferred_element_type=F32)


def back_term(grad, weight):
    return jnp.einsum("td,fd->tf", grad, weight, preferred_element_type=F32)


def forward_term(values, weight):
    return jnp.dot(values, weight, preferred_element_type=F32)


def column_sum(values):
    return jnp.sum(values.astype(F32), axis=0)


def mix_columns(values, spots, n):
    size = values.shape[1] // n
    return jnp.take(values, (spots[:, None] * size + jnp.arange(size)[None, :]).reshape(-1), axis=1)


def arrange(values, row_spots, col_spots, plain, mixed):
    n_rows, n_cols = row_spots.shape[0], col_spots.shape[0]
    height, width = values.shape[0] // n_rows, values.shape[1]
    size = width // n_cols
    if mixed and size % LANES:
        both = arrange(values, row_spots, col_spots, True, False)
        mix = (mix_columns(both[0], col_spots, n_cols),)
        return both + mix if plain else mix
    fan = n_rows // 2 if width * height * n_rows > (1 << 20) else n_rows

    def body(rows, cols, *refs):
        ins, outs = refs[:fan], list(refs[fan:])
        if plain:
            out = outs.pop(0)
            for k in range(fan):
                out[k * height : (k + 1) * height, :] = ins[k][...]
        if mixed:
            out = outs.pop(0)
            for k in range(fan):
                for p in range(n_cols):
                    place = pl.multiple_of(cols[p] * size, LANES)
                    out[k * height : (k + 1) * height, p * size : (p + 1) * size] = ins[k][:, pl.ds(place, size)]

    count = int(plain) + int(mixed)
    out = pl.pallas_call(
        body,
        out_shape=[jax.ShapeDtypeStruct(values.shape, values.dtype)] * count,
        grid_spec=pltpu.PrefetchScalarGridSpec(
            num_scalar_prefetch=2,
            grid=(n_rows // fan,),
            in_specs=[
                pl.BlockSpec((height, width), lambda i, rows, cols, k=k: (rows[i * fan + k], 0))
                for k in range(fan)
            ],
            out_specs=[pl.BlockSpec((fan * height, width), lambda i, rows, cols: (i, 0))] * count,
        ),
        name="arrange",
    )(row_spots, col_spots, *([values] * fan))
    return tuple(out)


def take_in(pieces, shared, part, col_spots, combine, earlier):
    count = len(pieces)
    height, width = pieces[0].shape
    n_cols = col_spots.shape[0]
    size = width // n_cols
    mixing = size % LANES == 0
    outputs = 2 if mixing else 1
    strip = height // 4

    def body(cols, *refs):
        ins, rest = refs[:count], refs[count:]
        extra = rest[: len(shared)]
        outs = rest[len(rest) - outputs :]
        for p in range(count):
            block = [e[0, p] if len(e.shape) == 4 else e[...] for e in extra]
            outs[0][0, p] = combine(ins[p][...], *block).astype(BF16)
            if mixing:
                for k in range(n_cols):
                    place = pl.multiple_of(cols[k] * size, LANES)
                    outs[1][0, p, :, k * size : (k + 1) * size] = outs[0][0, p, :, pl.ds(place, size)]

    rows_block = pl.BlockSpec((1, count, strip, width), lambda i, cols: (part, 0, i, 0))
    in_specs = [pl.BlockSpec((strip, width), lambda i, cols: (i, 0))] * count
    operands = list(pieces)
    for s in shared:
        if s.shape[0] == 1:
            in_specs.append(pl.BlockSpec((1, width), lambda i, cols: (0, 0)))
            operands.append(s)
        else:
            in_specs.append(rows_block)
            operands.append(s.reshape(PARTS, count, height, width))
    aliases = {}
    if earlier is not None:
        for k in range(outputs):
            aliases[1 + len(operands)] = k
            operands.append(earlier[k].reshape(PARTS, count, height, width))
            in_specs.append(pl.BlockSpec(memory_space=pl.ANY))
    out = pl.pallas_call(
        body,
        out_shape=[jax.ShapeDtypeStruct((PARTS, count, height, width), BF16)] * outputs,
        grid_spec=pltpu.PrefetchScalarGridSpec(
            num_scalar_prefetch=1,
            grid=(height // strip,),
            in_specs=in_specs,
            out_specs=[rows_block] * outputs,
        ),
        input_output_aliases=aliases,
        name="take_in",
    )(col_spots, *operands)
    return tuple(o.reshape(PARTS * count * height, width) for o in out), out[0]


def place_rows(pieces, row_spots, total_rows, earlier):
    count = len(pieces)
    height, width = pieces[0].shape

    def body(rows, *refs):
        i = pl.program_id(0)
        for p in range(count):

            @pl.when(i == p)
            def _():
                refs[-1][...] = refs[p][...]

    operands = list(pieces)
    in_specs = [pl.BlockSpec((height, width), lambda i, rows: (0, 0))] * count
    aliases = {}
    if earlier is not None:
        aliases[1 + count] = 0
        operands.append(earlier)
        in_specs.append(pl.BlockSpec(memory_space=pl.ANY))
    return pl.pallas_call(
        body,
        out_shape=jax.ShapeDtypeStruct((total_rows, width), F32),
        grid_spec=pltpu.PrefetchScalarGridSpec(
            num_scalar_prefetch=1,
            grid=(count,),
            in_specs=in_specs,
            out_specs=pl.BlockSpec((height, width), lambda i, rows: (rows[i], 0)),
        ),
        input_output_aliases=aliases,
        name="place_rows",
    )(row_spots, *operands)


def on_device(
    hidden_in,
    doc_ids,
    ln1_gain,
    ln1_bias,
    q_weight,
    q_bias,
    kv_weight,
    v_bias,
    o_weight,
    o_bias,
    ln2_gain,
    ln2_bias,
    up_weight,
    up_bias,
    down_weight,
    down_bias,
    cotangent,
):
    n_t = lax.axis_size("tensor")
    n_d = lax.axis_size("dp")
    assert n_t == 4 and n_d >= 4
    t = lax.axis_index("tensor")
    d = lax.axis_index("dp")
    rows_here, width = hidden_in.shape
    windows, length = doc_ids.shape
    head_dim = kv_weight.shape[1] // 2
    heads = q_weight.shape[1] // head_dim
    units = up_weight.shape[1]
    own_rows = rows_here // n_t
    piece = own_rows // PARTS
    part_rows = rows_here // PARTS

    t_order = [reverse_bits(p, n_t) for p in range(n_t)]
    part_spots = [jnp.stack([(t ^ k) * PARTS + c for k in t_order]).astype(jnp.int32) for c in range(PARTS)]
    row_spots = jnp.concatenate(part_spots)
    row_back = jnp.stack(
        [c * n_t + reverse_bits(t ^ j, n_t) for j in range(n_t) for c in range(PARTS)]
    ).astype(jnp.int32)
    row_same = jnp.arange(n_t * PARTS, dtype=jnp.int32)
    col_spots = jnp.stack([d ^ k for k in quarter_order(n_d)]).astype(jnp.int32)

    state = Store()
    steps = {}
    last = []

    def define(name):
        def put(fn):
            steps[name.replace(".", "_")] = fn
            return fn

        return put

    def hold(*values):
        if not last:
            return values if len(values) > 1 else values[0]
        out = lax.optimization_barrier(tuple(values) + (last[-1],))
        return out[:-1] if len(values) > 1 else out[0]

    def done(value):
        last[:] = [value]

    def part_of(values, c):
        return values[c * part_rows : (c + 1) * part_rows]

    @define(S.attn)
    def _():
        normed, _ = layer_norm(hidden_in.astype(F32))
        first_in = (normed * ln1_gain + ln1_bias).astype(BF16)
        queries = (forward_term(first_in, q_weight) + q_bias).astype(BF16)
        kv_shift = jnp.concatenate([jnp.zeros((head_dim,), F32), v_bias.astype(F32)])
        keyvals = (forward_term(first_in, kv_weight) + kv_shift).astype(BF16)
        q_all = queries.reshape(windows, length, heads, head_dim)
        k_all = keyvals[:, :head_dim].reshape(windows, length, head_dim)
        v_all = keyvals[:, head_dim:].reshape(windows, length, head_dim)
        attended = [attend_window(q_all[w], k_all[w], v_all[w], doc_ids[w]) for w in range(windows)]
        context = jnp.concatenate([a[0].reshape(length, heads * head_dim) for a in attended], axis=0)
        context = arrange(context.astype(BF16), row_spots, col_spots, True, False)[0]
        state.update(first_in=first_in, q=q_all, k=k_all, v=v_all, lse=[a[1] for a in attended])
        state.update(context=context)
        done(context)

    @define(S.cot)
    def _():
        state.cot, state.cot_cols = arrange(hold(cotangent), row_spots, col_spots, True, True)
        done(state.cot_cols)

    unit_step = units // CHUNKS

    for k in range(CHUNKS):
        here = slice(k * unit_step, (k + 1) * unit_step)

        @define(f"dh{k}")
        def _(k=k, here=here):
            state[f"dh{k}"] = back_term(hold(state.cot), down_weight[here])
            done(state[f"dh{k}"])

        @define(f"u{k}")
        def _(k=k, here=here):
            second = hold(state.second_pair[0])
            upper = forward_term(second, up_weight[:, here]) + up_bias[here]
            value, pull = jax.vjp(partial(jax.nn.gelu, approximate=True), upper)
            state[f"h{k}"] = value.astype(BF16)
            state[f"du{k}"] = pull(state[f"dh{k}"])[0].astype(BF16)
            done(state[f"h{k}"])

    @define(S.join)
    def _():
        parts = hold(*[state[f"{name}{k}"] for name in ("h", "du") for k in range(CHUNKS)])
        state.activ = jnp.concatenate(parts[:CHUNKS], axis=1)
        state.grad_upper = jnp.concatenate(parts[CHUNKS:], axis=1)
        state.up_sum = column_sum(state.grad_upper)
        done(state.grad_upper)

    @define(S.a1p)
    def _():
        state.first_cols = arrange(hold(state.first_in), row_same, col_spots, False, True)[0]
        done(state.first_cols)

    def row_sum(tag, values, multiply, c):
        low = c * part_rows
        middle = low + part_rows // 2

        @define(f"{tag}_s{c}")
        def _():
            sent = multiply(hold(values()[middle : middle + part_rows // 2]))
            state[f"{tag}_c{c}"] = swap(sent, "tensor", 1)
            done(sent)

        @define(f"{tag}_k{c}")
        def _():
            total = multiply(hold(values()[low:middle]))
            state[f"{tag}_kept{c}"] = total
            done(total)

        @define(f"{tag}_a{c}")
        def _():
            arrived = hold(state[f"{tag}_c{c}"])
            kept = state[f"{tag}_kept{c}"]
            sent = kept[piece:] + arrived[piece:]
            state[f"{tag}_near{c}"] = arrived
            state[f"{tag}_x{c}"] = swap(sent, "tensor", 2)
            done(sent)

    def own_sum(tag, c):
        arrived = hold(state[f"{tag}_x{c}"])
        return state[f"{tag}_kept{c}"][:piece] + state[f"{tag}_near{c}"][:piece] + arrived

    def spread(tag, values, c):
        state[f"{tag}{c}"] = values
        state[f"{tag}x{c}"] = swap(values, "tensor", 2)

    def pass_on(name, tag, c):
        @define(f"{name}{c}")
        def _():
            arrived = hold(state[f"{tag}x{c}"])
            state[f"{tag}x{c}"] = arrived
            state[f"{tag}c{c}"] = swap(state[f"{tag}{c}"], "tensor", 1)
            state[f"{tag}g{c}"] = swap(arrived, "tensor", 1)
            done(arrived)

    def pieces_of(tag, c):
        return hold(state[f"{tag}{c}"], state[f"{tag}x{c}"], state[f"{tag}c{c}"], state[f"{tag}g{c}"])

    own_in = lax.dynamic_slice_in_dim(hidden_in, t * own_rows, own_rows, 0)
    own_cot = lax.dynamic_slice_in_dim(cotangent, t * own_rows, own_rows, 0)

    def own_part(values, c):
        return values[c * piece : (c + 1) * piece].astype(F32)

    for c in range(PARTS):
        row_sum("ao", lambda: state.context, lambda v: forward_term(v, o_weight), c)

        @define(f"n{c}")
        def _(c=c):
            resid = own_part(own_in, c) + own_sum("ao", c) + o_bias
            plain, scale = layer_norm(resid)
            state[f"resid{c}"] = resid
            state[f"scale{c}"] = scale
            spread("n", plain, c)
            done(plain)

        pass_on("g", "n", c)

        @define(f"as{c}")
        def _(c=c):
            out, token = take_in(
                pieces_of("n", c),
                [ln2_gain.reshape(1, width), ln2_bias.reshape(1, width)],
                c,
                col_spots,
                lambda v, g, b: v * g.astype(F32) + b.astype(F32),
                state.get(S.second_pair),
            )
            state.second_pair = out
            done(token)

        row_sum("sp", lambda: state.grad_upper, lambda v: back_term(v, up_weight), c)
        row_sum("ff", lambda: state.activ, lambda v: forward_term(v, down_weight), c)

        @define(f"lo{c}")
        def _(c=c):
            state[f"out{c}"] = (state[f"resid{c}"] + own_sum("ff", c) + down_bias).astype(BF16)
            done(state[f"out{c}"])

        @define(f"b{c}")
        def _(c=c):
            grad_second = own_sum("sp", c)
            back, gain_grad, bias_grad = norm_back(
                grad_second, state[f"n{c}"], state[f"scale{c}"], ln2_gain
            )
            spread("b", back, c)
            state[f"grad_resid{c}"] = own_part(own_cot, c) + back
            state[f"ln2_{c}"] = (gain_grad, bias_grad)
            done(back)

        pass_on("gb", "b", c)

        @define(f"asb{c}")
        def _(c=c):
            out, token = take_in(
                pieces_of("b", c),
                [state.cot],
                c,
                col_spots,
                lambda v, g: g.astype(F32) + v,
                state.get(S.attn_pair),
            )
            state.attn_pair = out
            done(token)

        row_sum("fp", lambda: state.stack, lambda v: back_term(v, state.stack_w), c)

        @define(f"l{c}")
        def _(c=c):
            grad_first = own_sum("fp", c)
            plain, scale = layer_norm(own_part(own_in, c))
            back, gain_grad, bias_grad = norm_back(grad_first, plain, scale, ln1_gain)
            result = state[f"grad_resid{c}"] + back
            spread("l", result, c)
            state[f"ln1_{c}"] = (gain_grad, bias_grad)
            done(result)

        pass_on("gl", "l", c)

        @define(f"out{c}")
        def _(c=c):
            out = place_rows(pieces_of("l", c), part_spots[c], rows_here, state.get(S.input_grad))
            state.input_grad = out
            done(out)

    @define(S.abw)
    def _():
        grad_attn = hold(state.attn_pair[0])
        grad_context = back_term(grad_attn, o_weight).astype(BF16)
        grad_context = arrange(grad_context, row_back, col_spots, True, False)[0]
        grad_ctx_all = grad_context.reshape(windows, length, heads, head_dim)
        pulled = [
            attend_back(state.q[w], state.k[w], state.v[w], doc_ids[w], state.lse[w], grad_ctx_all[w])
            for w in range(windows)
        ]
        grad_query = jnp.concatenate(
            [p[0].reshape(length, heads * head_dim) for p in pulled], axis=0
        ).astype(BF16)
        kv_part = jnp.concatenate([jnp.concatenate([p[1], p[2]], axis=-1) for p in pulled], axis=0)
        high = kv_part.astype(BF16)
        low = (kv_part - high.astype(F32)).astype(BF16)
        stack = jnp.concatenate([grad_query, high, low], axis=1)
        state.grad_query = grad_query
        state.kv_terms = jnp.concatenate([high, low], axis=1)
        state.q_sum = column_sum(grad_query)
        state.v_sum = jnp.sum(kv_part[:, head_dim:], axis=0)
        state.stack = arrange(stack, row_spots, col_spots, True, False)[0]
        state.stack_w = jnp.concatenate([q_weight, kv_weight, kv_weight], axis=1)
        done(state.stack)

    half = width // 2
    quarter = width // 4

    def cut(values, lo, hi, axis):
        return lax.slice_in_dim(values, lo, hi, axis=axis)

    def tail(values, axis):
        middle = values.shape[axis] // 2
        return cut(values, 0, middle, axis), cut(values, middle, 2 * middle, axis)

    def finish(kept, sent_back, axis, bit):
        total = kept + sent_back
        while bit < n_d:
            kept, sent = tail(total, axis)
            total = kept + swap(sent, "dp", bit)
            bit *= 2
        return total

    def dims(axis, block, other):
        return (block, other) if axis == 0 else (other, block)

    def grad_low_first(tag, term, axis):
        @define(f"{tag}.s")
        def _():
            sent = term(half, width, hold)
            state[f"{tag}.y"] = swap(sent, "dp", 1)
            done(sent)

        @define(f"{tag}.q")
        def _():
            arrived = hold(state[f"{tag}.y"])
            total = term(quarter, half, lambda v: v) + cut(arrived, 0, quarter, axis)
            state[f"{tag}.rest"] = cut(arrived, quarter, half, axis)
            state[f"{tag}.z1"] = swap(total, "dp", 2)
            done(total)

        @define(f"{tag}.k")
        def _():
            arrived, rest = hold(state[f"{tag}.z1"], state[f"{tag}.rest"])
            total = term(0, quarter, lambda v: v) + rest + arrived
            kept, sent = tail(total, axis)
            state[f"{tag}.kept"] = kept
            state[f"{tag}.z2"] = swap(sent, "dp", 4)
            done(total)

        @define(f"{tag}.f")
        def _():
            arrived = hold(state[f"{tag}.z2"])
            state[tag] = finish(state[f"{tag}.kept"], arrived, axis, 8)
            done(state[tag])

    def grad_high_first(tag, term, axis):
        @define(f"{tag}.s")
        def _():
            sent = term(quarter, 3 * quarter, hold)
            state[f"{tag}.z1"] = swap(sent, "dp", 2)
            done(sent)

        @define(f"{tag}.q")
        def _():
            arrived = hold(state[f"{tag}.z1"])
            near = term(0, quarter, lambda v: v) + cut(arrived, 0, quarter, axis)
            far = term(3 * quarter, width, lambda v: v) + cut(arrived, quarter, half, axis)
            near, near_sent = tail(near, axis)
            far, far_sent = tail(far, axis)
            sent = jnp.concatenate([near_sent, far_sent], axis=axis)
            state[f"{tag}.kept"] = (near, far)
            state[f"{tag}.z2"] = swap(sent, "dp", 4)
            done(sent)

        @define(f"{tag}.k")
        def _():
            arrived = hold(state[f"{tag}.z2"])
            near, far = state[f"{tag}.kept"]
            a, b = tail(arrived, axis)
            near = finish(near, a, axis, 8)
            far = finish(far, b, axis, 8)
            state[f"{tag}.kept"] = near
            state[f"{tag}.y"] = swap(far, "dp", 1)
            done(far)

        @define(f"{tag}.f")
        def _():
            arrived = hold(state[f"{tag}.y"])
            state[tag] = state[f"{tag}.kept"] + arrived
            done(state[tag])

    def mixed_of(pair_name):
        pair = state[pair_name]
        return pair[1] if len(pair) > 1 else mix_columns(pair[0], col_spots, n_d)

    def rows_term(left, right):
        def term(lo, hi, h):
            return over_tokens(h(left()[:, lo:hi]), right())

        return term

    def cols_term(left, right):
        def term(lo, hi, h):
            return over_tokens(left(), h(right()[:, lo:hi]))

        return term

    def piece_of(get, k, n):
        def f():
            values = get()
            size = values.shape[1] // n
            return values[:, k * size : (k + 1) * size]

        return f

    for name in ORDER:
        if not name.endswith("_s") or name.startswith("kv"):
            continue
        tag = name[:-2]
        kind, index = tag[:2], tag[2:]
        k, n, high = int(index[0]), int(index[1]), index.endswith("z")
        make = grad_high_first if high else grad_low_first
        if kind == "dn":
            make(tag, cols_term(lambda k=k: state[f"h{k}"], lambda: state.cot_cols), 1)
        elif kind == "up":
            make(tag, rows_term(lambda: mixed_of("second_pair"), lambda k=k: state[f"du{k}"]), 0)
        elif kind == "oo":
            make(tag, cols_term(piece_of(lambda: state.context, k, n), lambda: mixed_of("attn_pair")), 1)
        else:
            make(tag, rows_term(lambda: state.first_cols, piece_of(lambda: state.grad_query, k, n)), 0)

    def joined(kind, axis):
        found = sorted(name[:-2] for name in ORDER if name.startswith(kind) and name.endswith("_s"))
        return jnp.concatenate([state[tag] for tag in found], axis=axis)

    share = width // (n_d * n_t)

    @define(S.kv_m)
    def _():
        pair = over_tokens(hold(state.first_cols), state.kv_terms)
        term = (pair[:, : 2 * head_dim] + pair[:, 2 * head_dim :]).reshape(n_d, 2, 2, share, 2 * head_dim)
        core = t & 1
        sent = lax.dynamic_index_in_dim(term, 1 - core, 2, keepdims=False)
        state.kv_keep = lax.dynamic_index_in_dim(term, core, 2, keepdims=False)
        state.kv_c = swap(sent, "tensor", 1)
        done(sent)

    @define(S.kv_x)
    def _():
        total = state.kv_keep + hold(state.kv_c)
        chip = t >> 1
        sent = lax.dynamic_index_in_dim(total, 1 - chip, 1, keepdims=False)
        state.kv_keep = lax.dynamic_index_in_dim(total, chip, 1, keepdims=False)
        state.kv_xx = swap(sent, "tensor", 2)
        done(sent)

    @define(S.kv_s)
    def _():
        total = (state.kv_keep + hold(state.kv_xx)).reshape(n_d * share, 2 * head_dim)
        quart = n_d * share // 4
        state.kv_q1, state.kv_q0 = total[quart : 2 * quart], total[:quart]
        sent = total[2 * quart :]
        state.kv_y = swap(sent, "dp", 1)
        done(sent)

    @define(S.kv_q)
    def _():
        arrived = hold(state.kv_y)
        quart = n_d * share // 4
        sent = state.kv_q1 + arrived[:quart]
        state.kv_q0 = state.kv_q0 + arrived[quart:]
        state.kv_z1 = swap(sent, "dp", 2)
        done(sent)

    @define(S.kv_k)
    def _():
        total = state.kv_q0 + hold(state.kv_z1)
        kept, sent = tail(total, 0)
        state.kv_keep = kept
        state.kv_z2 = swap(sent, "dp", 4)
        done(total)

    @define(S.kv_f)
    def _():
        total = finish(state.kv_keep, hold(state.kv_z2), 0, 8)
        spread("kv", total, 0)
        done(total)

    pass_on("kv.g", "kv", 0)

    @define(S.kv_o)
    def _():
        own, other_x, other_c, other_cx = pieces_of("kv", 0)
        core, chip = t & 1, t >> 1
        pair = jnp.where(core == 0, jnp.stack([own, other_c]), jnp.stack([other_c, own]))
        pair_x = jnp.where(core == 0, jnp.stack([other_x, other_cx]), jnp.stack([other_cx, other_x]))
        whole = jnp.where(chip == 0, jnp.stack([pair, pair_x]), jnp.stack([pair_x, pair]))
        state.kv_grad = whole.reshape(n_t * share, 2 * head_dim)
        done(state.kv_grad)

    @define(S.v_0)
    def _():
        resid = jnp.concatenate([state[f"grad_resid{c}"] for c in range(PARTS)], axis=0)
        values = jnp.concatenate(
            [
                state.ln1_0[0] + state.ln1_1[0],
                state.ln1_0[1] + state.ln1_1[1],
                column_sum(resid.astype(BF16)),
                state.ln2_0[0] + state.ln2_1[0],
                state.ln2_0[1] + state.ln2_1[1],
                column_sum(own_cot),
                state.v_sum,
            ]
        )
        values = hold(values)
        state.v = values
        state.v_c = swap(values, "tensor", 1)
        done(values)

    @define(S.v_1)
    def _():
        state.v = state.v + hold(state.v_c)
        state.v_x = swap(state.v, "tensor", 2)
        done(state.v)

    @define(S.v_2)
    def _():
        total = state.v + hold(state.v_x)
        up_sum = state.up_sum
        state.v = jnp.concatenate([total, state.q_sum, up_sum])
        state.v_y = swap(state.v, "dp", 1)
        done(state.v)

    @define(S.v_3)
    def _():
        state.v = state.v + hold(state.v_y)
        state.v_z1 = swap(state.v, "dp", 2)
        done(state.v)

    @define(S.v_4)
    def _():
        state.v = state.v + hold(state.v_z1)
        state.v_z2 = swap(state.v, "dp", 4)
        done(state.v)

    @define(S.v_5)
    def _():
        total = state.v + hold(state.v_z2)
        bit = 8
        while bit < n_d:
            total = total + swap(total, "dp", bit)
            bit *= 2
        state.v = total
        done(total)

    for name in ORDER:
        with jax.named_scope("step." + name):
            steps[name]()

    vectors = []
    place = 0
    for size in (width,) * 6 + (head_dim, heads * head_dim, units):
        vectors.append(state.v[place : place + size])
        place += size
    return (
        jnp.concatenate([state.out0, state.out1], axis=0),
        state.input_grad,
        vectors[0],
        vectors[1],
        joined("qq", 1),
        vectors[7],
        state.kv_grad,
        vectors[6],
        joined("oo", 0),
        vectors[2],
        vectors[3],
        vectors[4],
        joined("up", 1),
        vectors[8],
        joined("dn", 0),
        vectors[5],
    )


def solution(mesh):
    in_specs = (
        P("dp", None),
        P("dp", None),
        P(),
        P(),
        P(None, "tensor"),
        P("tensor"),
        P(),
        P(),
        P("tensor", None),
        P(),
        P(),
        P(),
        P(None, "tensor"),
        P("tensor"),
        P("tensor", None),
        P(),
        P("dp", None),
    )
    out_specs = (
        P(("dp", "tensor"), None),
        P("dp", None),
        P(),
        P(),
        P("dp", "tensor"),
        P("tensor"),
        P("dp", None),
        P(),
        P("tensor", "dp"),
        P(),
        P(),
        P(),
        P("dp", "tensor"),
        P("tensor"),
        P("tensor", "dp"),
        P(),
    )
    return jax.shard_map(
        on_device, mesh=mesh, in_specs=in_specs, out_specs=out_specs, check_vma=False
    )
```

```python
from functools import partial

import jax
import jax.numpy as jnp
from jax import lax
from jax.experimental import pallas as pl
from jax.experimental.pallas import tpu as pltpu
from jax.sharding import PartitionSpec as P

EPS = 1e-05
F32 = jnp.float32
BF16 = jnp.bfloat16
CHUNKS = 4
PARTS = 2
LANES = 128

class Names:
    def __getattr__(self, name):
        return name


class Store(dict):
    __getattr__ = dict.__getitem__
    __setattr__ = dict.__setitem__


S = Names()

ORDER = (
    S.attn, S.ao_s1, S.ao_k0, S.ao_k1, S.cot, S.ao_s0, S.ao_a1, S.dh3, S.dh2, S.ao_a0, S.dh0, S.dh1, S.n1,
    S.a1p, S.n0, S.g1, S.g0, S.as1, S.as0, S.u1, S.dn14z_s, S.up14_s, S.u0, S.dn04_s, S.u2, S.u3, S.join,
    S.sp_s0, S.ff_k1, S.dn14z_q, S.ff_s1, S.up14_q, S.ff_k0, S.sp_k0, S.ff_a1, S.sp_a0, S.sp_k1, S.dn14z_k,
    S.up14_k, S.dn04_q, S.dn14z_f, S.dn34_s, S.lo1, S.sp_s1, S.b0, S.up14_f, S.up04_s, S.dn04_k, S.sp_a1,
    S.dn34_q, S.dn04_f, S.gb0, S.b1, S.dn34_k, S.asb0, S.up24_s, S.gb1, S.up04_q, S.dn34_f, S.up34_s,
    S.asb1, S.up04_k, S.abw, S.fp_s0, S.up24_q, S.oo01_s, S.fp_k0, S.fp_a0, S.fp_k1, S.up04_f, S.ff_s0,
    S.up24_k, S.up34_q, S.ff_a0, S.l0, S.up24_f, S.qq12_s, S.lo0, S.up34_k, S.oo01_q, S.dn24_s, S.up34_f,
    S.gl0, S.oo01_k, S.qq12_q, S.out0, S.kv_m, S.fp_s1, S.oo01_f, S.qq12_k, S.qq02z_s, S.kv_x, S.fp_a1,
    S.qq12_f, S.kv_s, S.qq02z_q, S.kv_q, S.l1, S.v_0, S.qq02z_k, S.kv_k, S.dn24_q, S.v_1, S.qq02z_f, S.gl1,
    S.kv_f, S.v_2, S.dn24_k, S.v_3, S.out1, S.kv_g0, S.dn24_f, S.v_4, S.kv_o, S.v_5,
)


def reverse_bits(value, n):
    bits = n.bit_length() - 1
    assert 1 << bits == n
    out = 0
    for b in range(bits):
        out = out | (((value >> b) & 1) << (bits - 1 - b))
    return out


def quarter_order(n):
    rest = n // 4
    return [low + 4 * reverse_bits(i, rest) for low in (0, 2, 3, 1) for i in range(rest)]


def swap(values, axis_name, bit):
    n = lax.axis_size(axis_name)
    return lax.ppermute(values, axis_name, [(i, i ^ bit) for i in range(n)])


def layer_norm(values):
    mean_row = jnp.mean(values, axis=-1, keepdims=True)
    centred = values - mean_row
    inv_scale = lax.rsqrt(jnp.mean(centred * centred, axis=-1, keepdims=True) + EPS)
    return (centred * inv_scale, inv_scale)


def norm_back(grad_out, normed, inv_scale, gain):
    scaled = grad_out * gain
    inner = (
        scaled
        - jnp.mean(scaled, axis=-1, keepdims=True)
        - normed * jnp.mean(scaled * normed, axis=-1, keepdims=True)
    )
    return (inner * inv_scale, jnp.sum(grad_out * normed, axis=0), jnp.sum(grad_out, axis=0))


def visible_mask(ids_win, start, finish):
    query_pos = start + jnp.arange(finish - start)
    key_pos = jnp.arange(finish)
    same_doc = ids_win[start:finish][:, None] == ids_win[:finish][None, :]
    return (key_pos[None, :] <= query_pos[:, None]) & same_doc


def attend_window(q_win, k_win, v_win, ids_win):
    length = ids_win.shape[0]
    block = min(512, length)
    factor = q_win.shape[-1] ** (-0.5)
    outs = []
    sums = []
    for start in range(0, length, block):
        finish = start + block
        scores = (
            jnp.einsum("qhd,kd->hqk", q_win[start:finish], k_win[:finish], preferred_element_type=F32)
            * factor
        )
        visible = visible_mask(ids_win, start, finish)
        scores = jnp.where(visible[None], scores, -1e30)
        peak = jnp.max(scores, axis=-1, keepdims=True)
        expo = jnp.exp(scores - peak)
        total = jnp.sum(expo, axis=-1, keepdims=True)
        probs = (expo / total).astype(BF16)
        outs.append(jnp.einsum("hqk,kd->qhd", probs, v_win[:finish], preferred_element_type=F32))
        sums.append((peak + jnp.log(total))[..., 0])
    return (jnp.concatenate(outs, axis=0), jnp.concatenate(sums, axis=1))


def attend_back(q_win, k_win, v_win, ids_win, lse_win, grad_win):
    length = ids_win.shape[0]
    head_dim = k_win.shape[-1]
    block = min(512, length)
    factor = head_dim ** (-0.5)
    grad_q_parts = []
    grad_keys = jnp.zeros((length, head_dim), F32)
    grad_vals = jnp.zeros((length, head_dim), F32)
    for start in range(0, length, block):
        finish = start + block
        q_part = q_win[start:finish]
        grad_part = grad_win[start:finish]
        scores = (
            jnp.einsum("qhd,kd->hqk", q_part, k_win[:finish], preferred_element_type=F32) * factor
        )
        visible = visible_mask(ids_win, start, finish)
        probs = jnp.where(visible[None], jnp.exp(scores - lse_win[:, start:finish, None]), 0.0)
        grad_probs = jnp.einsum("qhd,kd->hqk", grad_part, v_win[:finish], preferred_element_type=F32)
        grad_vals = grad_vals.at[:finish].add(
            jnp.einsum("hqk,qhd->kd", probs.astype(BF16), grad_part, preferred_element_type=F32)
        )
        delta = jnp.sum(probs * grad_probs, axis=-1, keepdims=True)
        grad_scores = (probs * (grad_probs - delta)).astype(BF16)
        grad_q_parts.append(
            jnp.einsum("hqk,kd->qhd", grad_scores, k_win[:finish], preferred_element_type=F32) * factor
        )
        grad_keys = grad_keys.at[:finish].add(
            jnp.einsum("hqk,qhd->kd", grad_scores, q_part, preferred_element_type=F32) * factor
        )
    return (jnp.concatenate(grad_q_parts, axis=0), grad_keys, grad_vals)


def over_tokens(left, right):
    return jnp.einsum("tf,td->fd", left, right, preferred_element_type=F32)


def back_term(grad, weight):
    return jnp.einsum("td,fd->tf", grad, weight, preferred_element_type=F32)


def forward_term(values, weight):
    return jnp.dot(values, weight, preferred_element_type=F32)


def column_sum(values):
    return jnp.sum(values.astype(F32), axis=0)


def mix_columns(values, spots, n):
    size = values.shape[1] // n
    return jnp.take(values, (spots[:, None] * size + jnp.arange(size)[None, :]).reshape(-1), axis=1)


def arrange(values, row_spots, col_spots, plain, mixed):
    n_rows, n_cols = row_spots.shape[0], col_spots.shape[0]
    height, width = values.shape[0] // n_rows, values.shape[1]
    size = width // n_cols
    if mixed and size % LANES:
        both = arrange(values, row_spots, col_spots, True, False)
        mix = (mix_columns(both[0], col_spots, n_cols),)
        return both + mix if plain else mix
    fan = n_rows // 2 if width * height * n_rows > (1 << 20) else n_rows

    def body(rows, cols, *refs):
        ins, outs = refs[:fan], list(refs[fan:])
        if plain:
            out = outs.pop(0)
            for k in range(fan):
                out[k * height : (k + 1) * height, :] = ins[k][...]
        if mixed:
            out = outs.pop(0)
            for k in range(fan):
                for p in range(n_cols):
                    place = pl.multiple_of(cols[p] * size, LANES)
                    out[k * height : (k + 1) * height, p * size : (p + 1) * size] = ins[k][:, pl.ds(place, size)]

    count = int(plain) + int(mixed)
    out = pl.pallas_call(
        body,
        out_shape=[jax.ShapeDtypeStruct(values.shape, values.dtype)] * count,
        grid_spec=pltpu.PrefetchScalarGridSpec(
            num_scalar_prefetch=2,
            grid=(n_rows // fan,),
            in_specs=[
                pl.BlockSpec((height, width), lambda i, rows, cols, k=k: (rows[i * fan + k], 0))
                for k in range(fan)
            ],
            out_specs=[pl.BlockSpec((fan * height, width), lambda i, rows, cols: (i, 0))] * count,
        ),
        name="arrange",
    )(row_spots, col_spots, *([values] * fan))
    return tuple(out)


def take_in(pieces, shared, part, col_spots, combine, earlier):
    count = len(pieces)
    height, width = pieces[0].shape
    n_cols = col_spots.shape[0]
    size = width // n_cols
    mixing = size % LANES == 0
    outputs = 2 if mixing else 1
    strip = height // 4

    def body(cols, *refs):
        ins, rest = refs[:count], refs[count:]
        extra = rest[: len(shared)]
        outs = rest[len(rest) - outputs :]
        for p in range(count):
            block = [e[0, p] if len(e.shape) == 4 else e[...] for e in extra]
            outs[0][0, p] = combine(ins[p][...], *block).astype(BF16)
            if mixing:
                for k in range(n_cols):
                    place = pl.multiple_of(cols[k] * size, LANES)
                    outs[1][0, p, :, k * size : (k + 1) * size] = outs[0][0, p, :, pl.ds(place, size)]

    rows_block = pl.BlockSpec((1, count, strip, width), lambda i, cols: (part, 0, i, 0))
    in_specs = [pl.BlockSpec((strip, width), lambda i, cols: (i, 0))] * count
    operands = list(pieces)
    for s in shared:
        if s.shape[0] == 1:
            in_specs.append(pl.BlockSpec((1, width), lambda i, cols: (0, 0)))
            operands.append(s)
        else:
            in_specs.append(rows_block)
            operands.append(s.reshape(PARTS, count, height, width))
    aliases = {}
    if earlier is not None:
        for k in range(outputs):
            aliases[1 + len(operands)] = k
            operands.append(earlier[k].reshape(PARTS, count, height, width))
            in_specs.append(pl.BlockSpec(memory_space=pl.ANY))
    out = pl.pallas_call(
        body,
        out_shape=[jax.ShapeDtypeStruct((PARTS, count, height, width), BF16)] * outputs,
        grid_spec=pltpu.PrefetchScalarGridSpec(
            num_scalar_prefetch=1,
            grid=(height // strip,),
            in_specs=in_specs,
            out_specs=[rows_block] * outputs,
        ),
        input_output_aliases=aliases,
        name="take_in",
    )(col_spots, *operands)
    return tuple(o.reshape(PARTS * count * height, width) for o in out), out[0]


def place_rows(pieces, row_spots, total_rows, earlier):
    count = len(pieces)
    height, width = pieces[0].shape

    def body(rows, *refs):
        i = pl.program_id(0)
        for p in range(count):

            @pl.when(i == p)
            def _():
                refs[-1][...] = refs[p][...]

    operands = list(pieces)
    in_specs = [pl.BlockSpec((height, width), lambda i, rows: (0, 0))] * count
    aliases = {}
    if earlier is not None:
        aliases[1 + count] = 0
        operands.append(earlier)
        in_specs.append(pl.BlockSpec(memory_space=pl.ANY))
    return pl.pallas_call(
        body,
        out_shape=jax.ShapeDtypeStruct((total_rows, width), F32),
        grid_spec=pltpu.PrefetchScalarGridSpec(
            num_scalar_prefetch=1,
            grid=(count,),
            in_specs=in_specs,
            out_specs=pl.BlockSpec((height, width), lambda i, rows: (rows[i], 0)),
        ),
        input_output_aliases=aliases,
        name="place_rows",
    )(row_spots, *operands)


def on_device(
    hidden_in,
    doc_ids,
    ln1_gain,
    ln1_bias,
    q_weight,
    q_bias,
    kv_weight,
    v_bias,
    o_weight,
    o_bias,
    ln2_gain,
    ln2_bias,
    up_weight,
    up_bias,
    down_weight,
    down_bias,
    cotangent,
):
    n_t = lax.axis_size("tensor")
    n_d = lax.axis_size("dp")
    assert n_t == 4 and n_d >= 4
    t = lax.axis_index("tensor")
    d = lax.axis_index("dp")
    rows_here, width = hidden_in.shape
    windows, length = doc_ids.shape
    head_dim = kv_weight.shape[1] // 2
    heads = q_weight.shape[1] // head_dim
    units = up_weight.shape[1]
    own_rows = rows_here // n_t
    piece = own_rows // PARTS
    part_rows = rows_here // PARTS

    t_order = [reverse_bits(p, n_t) for p in range(n_t)]
    part_spots = [jnp.stack([(t ^ k) * PARTS + c for k in t_order]).astype(jnp.int32) for c in range(PARTS)]
    row_spots = jnp.concatenate(part_spots)
    row_back = jnp.stack(
        [c * n_t + reverse_bits(t ^ j, n_t) for j in range(n_t) for c in range(PARTS)]
    ).astype(jnp.int32)
    row_same = jnp.arange(n_t * PARTS, dtype=jnp.int32)
    col_spots = jnp.stack([d ^ k for k in quarter_order(n_d)]).astype(jnp.int32)

    state = Store()
    steps = {}
    last = []

    def define(name):
        def put(fn):
            steps[name.replace(".", "_")] = fn
            return fn

        return put

    def hold(*values):
        if not last:
            return values if len(values) > 1 else values[0]
        out = lax.optimization_barrier(tuple(values) + (last[-1],))
        return out[:-1] if len(values) > 1 else out[0]

    def done(value):
        last[:] = [value]

    def part_of(values, c):
        return values[c * part_rows : (c + 1) * part_rows]

    @define(S.attn)
    def _():
        normed, _ = layer_norm(hidden_in.astype(F32))
        first_in = (normed * ln1_gain + ln1_bias).astype(BF16)
        queries = (forward_term(first_in, q_weight) + q_bias).astype(BF16)
        kv_shift = jnp.concatenate([jnp.zeros((head_dim,), F32), v_bias.astype(F32)])
        keyvals = (forward_term(first_in, kv_weight) + kv_shift).astype(BF16)
        q_all = queries.reshape(windows, length, heads, head_dim)
        k_all = keyvals[:, :head_dim].reshape(windows, length, head_dim)
        v_all = keyvals[:, head_dim:].reshape(windows, length, head_dim)
        attended = [attend_window(q_all[w], k_all[w], v_all[w], doc_ids[w]) for w in range(windows)]
        context = jnp.concatenate([a[0].reshape(length, heads * head_dim) for a in attended], axis=0)
        context = arrange(context.astype(BF16), row_spots, col_spots, True, False)[0]
        state.update(first_in=first_in, q=q_all, k=k_all, v=v_all, lse=[a[1] for a in attended])
        state.update(context=context)
        done(context)

    @define(S.cot)
    def _():
        state.cot, state.cot_cols = arrange(hold(cotangent), row_spots, col_spots, True, True)
        done(state.cot_cols)

    unit_step = units // CHUNKS

    for k in range(CHUNKS):
        here = slice(k * unit_step, (k + 1) * unit_step)

        @define(f"dh{k}")
        def _(k=k, here=here):
            state[f"dh{k}"] = back_term(hold(state.cot), down_weight[here])
            done(state[f"dh{k}"])

        @define(f"u{k}")
        def _(k=k, here=here):
            second = hold(state.second_pair[0])
            upper = forward_term(second, up_weight[:, here]) + up_bias[here]
            value, pull = jax.vjp(partial(jax.nn.gelu, approximate=True), upper)
            state[f"h{k}"] = value.astype(BF16)
            state[f"du{k}"] = pull(state[f"dh{k}"])[0].astype(BF16)
            done(state[f"h{k}"])

    @define(S.join)
    def _():
        parts = hold(*[state[f"{name}{k}"] for name in ("h", "du") for k in range(CHUNKS)])
        state.activ = jnp.concatenate(parts[:CHUNKS], axis=1)
        state.grad_upper = jnp.concatenate(parts[CHUNKS:], axis=1)
        state.up_sum = column_sum(state.grad_upper)
        done(state.grad_upper)

    @define(S.a1p)
    def _():
        state.first_cols = arrange(hold(state.first_in), row_same, col_spots, False, True)[0]
        done(state.first_cols)

    def row_sum(tag, values, multiply, c):
        low = c * part_rows
        middle = low + part_rows // 2

        @define(f"{tag}_s{c}")
        def _():
            sent = multiply(hold(values()[middle : middle + part_rows // 2]))
            state[f"{tag}_c{c}"] = swap(sent, "tensor", 1)
            done(sent)

        @define(f"{tag}_k{c}")
        def _():
            total = multiply(hold(values()[low:middle]))
            state[f"{tag}_kept{c}"] = total
            done(total)

        @define(f"{tag}_a{c}")
        def _():
            arrived = hold(state[f"{tag}_c{c}"])
            kept = state[f"{tag}_kept{c}"]
            sent = kept[piece:] + arrived[piece:]
            state[f"{tag}_near{c}"] = arrived
            state[f"{tag}_x{c}"] = swap(sent, "tensor", 2)
            done(sent)

    def own_sum(tag, c):
        arrived = hold(state[f"{tag}_x{c}"])
        return state[f"{tag}_kept{c}"][:piece] + state[f"{tag}_near{c}"][:piece] + arrived

    def spread(tag, values, c):
        state[f"{tag}{c}"] = values
        state[f"{tag}x{c}"] = swap(values, "tensor", 2)

    def pass_on(name, tag, c):
        @define(f"{name}{c}")
        def _():
            arrived = hold(state[f"{tag}x{c}"])
            state[f"{tag}x{c}"] = arrived
            state[f"{tag}c{c}"] = swap(state[f"{tag}{c}"], "tensor", 1)
            state[f"{tag}g{c}"] = swap(arrived, "tensor", 1)
            done(arrived)

    def pieces_of(tag, c):
        return hold(state[f"{tag}{c}"], state[f"{tag}x{c}"], state[f"{tag}c{c}"], state[f"{tag}g{c}"])

    own_in = lax.dynamic_slice_in_dim(hidden_in, t * own_rows, own_rows, 0)
    own_cot = lax.dynamic_slice_in_dim(cotangent, t * own_rows, own_rows, 0)

    def own_part(values, c):
        return values[c * piece : (c + 1) * piece].astype(F32)

    for c in range(PARTS):
        row_sum("ao", lambda: state.context, lambda v: forward_term(v, o_weight), c)

        @define(f"n{c}")
        def _(c=c):
            resid = own_part(own_in, c) + own_sum("ao", c) + o_bias
            plain, scale = layer_norm(resid)
            state[f"resid{c}"] = resid
            state[f"scale{c}"] = scale
            spread("n", plain, c)
            done(plain)

        pass_on("g", "n", c)

        @define(f"as{c}")
        def _(c=c):
            out, token = take_in(
                pieces_of("n", c),
                [ln2_gain.reshape(1, width), ln2_bias.reshape(1, width)],
                c,
                col_spots,
                lambda v, g, b: v * g.astype(F32) + b.astype(F32),
                state.get(S.second_pair),
            )
            state.second_pair = out
            done(token)

        row_sum("sp", lambda: state.grad_upper, lambda v: back_term(v, up_weight), c)
        row_sum("ff", lambda: state.activ, lambda v: forward_term(v, down_weight), c)

        @define(f"lo{c}")
        def _(c=c):
            state[f"out{c}"] = (state[f"resid{c}"] + own_sum("ff", c) + down_bias).astype(BF16)
            done(state[f"out{c}"])

        @define(f"b{c}")
        def _(c=c):
            grad_second = own_sum("sp", c)
            back, gain_grad, bias_grad = norm_back(
                grad_second, state[f"n{c}"], state[f"scale{c}"], ln2_gain
            )
            spread("b", back, c)
            state[f"grad_resid{c}"] = own_part(own_cot, c) + back
            state[f"ln2_{c}"] = (gain_grad, bias_grad)
            done(back)

        pass_on("gb", "b", c)

        @define(f"asb{c}")
        def _(c=c):
            out, token = take_in(
                pieces_of("b", c),
                [state.cot],
                c,
                col_spots,
                lambda v, g: g.astype(F32) + v,
                state.get(S.attn_pair),
            )
            state.attn_pair = out
            done(token)

        row_sum("fp", lambda: state.stack, lambda v: back_term(v, state.stack_w), c)

        @define(f"l{c}")
        def _(c=c):
            grad_first = own_sum("fp", c)
            plain, scale = layer_norm(own_part(own_in, c))
            back, gain_grad, bias_grad = norm_back(grad_first, plain, scale, ln1_gain)
            result = state[f"grad_resid{c}"] + back
            spread("l", result, c)
            state[f"ln1_{c}"] = (gain_grad, bias_grad)
            done(result)

        pass_on("gl", "l", c)

        @define(f"out{c}")
        def _(c=c):
            out = place_rows(pieces_of("l", c), part_spots[c], rows_here, state.get(S.input_grad))
            state.input_grad = out
            done(out)

    @define(S.abw)
    def _():
        grad_attn = hold(state.attn_pair[0])
        grad_context = back_term(grad_attn, o_weight).astype(BF16)
        grad_context = arrange(grad_context, row_back, col_spots, True, False)[0]
        grad_ctx_all = grad_context.reshape(windows, length, heads, head_dim)
        pulled = [
            attend_back(state.q[w], state.k[w], state.v[w], doc_ids[w], state.lse[w], grad_ctx_all[w])
            for w in range(windows)
        ]
        grad_query = jnp.concatenate(
            [p[0].reshape(length, heads * head_dim) for p in pulled], axis=0
        ).astype(BF16)
        kv_part = jnp.concatenate([jnp.concatenate([p[1], p[2]], axis=-1) for p in pulled], axis=0)
        high = kv_part.astype(BF16)
        low = (kv_part - high.astype(F32)).astype(BF16)
        stack = jnp.concatenate([grad_query, high, low], axis=1)
        state.grad_query = grad_query
        state.kv_terms = jnp.concatenate([high, low], axis=1)
        state.q_sum = column_sum(grad_query)
        state.v_sum = jnp.sum(kv_part[:, head_dim:], axis=0)
        state.stack = arrange(stack, row_spots, col_spots, True, False)[0]
        state.stack_w = jnp.concatenate([q_weight, kv_weight, kv_weight], axis=1)
        done(state.stack)

    half = width // 2
    quarter = width // 4

    def cut(values, lo, hi, axis):
        return lax.slice_in_dim(values, lo, hi, axis=axis)

    def tail(values, axis):
        middle = values.shape[axis] // 2
        return cut(values, 0, middle, axis), cut(values, middle, 2 * middle, axis)

    def finish(kept, sent_back, axis, bit):
        total = kept + sent_back
        while bit < n_d:
            kept, sent = tail(total, axis)
            total = kept + swap(sent, "dp", bit)
            bit *= 2
        return total

    def dims(axis, block, other):
        return (block, other) if axis == 0 else (other, block)

    def grad_low_first(tag, term, axis):
        @define(f"{tag}.s")
        def _():
            sent = term(half, width, hold)
            state[f"{tag}.y"] = swap(sent, "dp", 1)
            done(sent)

        @define(f"{tag}.q")
        def _():
            arrived = hold(state[f"{tag}.y"])
            total = term(quarter, half, lambda v: v) + cut(arrived, 0, quarter, axis)
            state[f"{tag}.rest"] = cut(arrived, quarter, half, axis)
            state[f"{tag}.z1"] = swap(total, "dp", 2)
            done(total)

        @define(f"{tag}.k")
        def _():
            arrived, rest = hold(state[f"{tag}.z1"], state[f"{tag}.rest"])
            total = term(0, quarter, lambda v: v) + rest + arrived
            kept, sent = tail(total, axis)
            state[f"{tag}.kept"] = kept
            state[f"{tag}.z2"] = swap(sent, "dp", 4)
            done(total)

        @define(f"{tag}.f")
        def _():
            arrived = hold(state[f"{tag}.z2"])
            state[tag] = finish(state[f"{tag}.kept"], arrived, axis, 8)
            done(state[tag])

    def grad_high_first(tag, term, axis):
        @define(f"{tag}.s")
        def _():
            sent = term(quarter, 3 * quarter, hold)
            state[f"{tag}.z1"] = swap(sent, "dp", 2)
            done(sent)

        @define(f"{tag}.q")
        def _():
            arrived = hold(state[f"{tag}.z1"])
            near = term(0, quarter, lambda v: v) + cut(arrived, 0, quarter, axis)
            far = term(3 * quarter, width, lambda v: v) + cut(arrived, quarter, half, axis)
            near, near_sent = tail(near, axis)
            far, far_sent = tail(far, axis)
            sent = jnp.concatenate([near_sent, far_sent], axis=axis)
            state[f"{tag}.kept"] = (near, far)
            state[f"{tag}.z2"] = swap(sent, "dp", 4)
            done(sent)

        @define(f"{tag}.k")
        def _():
            arrived = hold(state[f"{tag}.z2"])
            near, far = state[f"{tag}.kept"]
            a, b = tail(arrived, axis)
            near = finish(near, a, axis, 8)
            far = finish(far, b, axis, 8)
            state[f"{tag}.kept"] = near
            state[f"{tag}.y"] = swap(far, "dp", 1)
            done(far)

        @define(f"{tag}.f")
        def _():
            arrived = hold(state[f"{tag}.y"])
            state[tag] = state[f"{tag}.kept"] + arrived
            done(state[tag])

    def mixed_of(pair_name):
        pair = state[pair_name]
        return pair[1] if len(pair) > 1 else mix_columns(pair[0], col_spots, n_d)

    def rows_term(left, right):
        def term(lo, hi, h):
            return over_tokens(h(left()[:, lo:hi]), right())

        return term

    def cols_term(left, right):
        def term(lo, hi, h):
            return over_tokens(left(), h(right()[:, lo:hi]))

        return term

    def piece_of(get, k, n):
        def f():
            values = get()
            size = values.shape[1] // n
            return values[:, k * size : (k + 1) * size]

        return f

    for name in ORDER:
        if not name.endswith("_s") or name.startswith("kv"):
            continue
        tag = name[:-2]
        kind, index = tag[:2], tag[2:]
        k, n, high = int(index[0]), int(index[1]), index.endswith("z")
        make = grad_high_first if high else grad_low_first
        if kind == "dn":
            make(tag, cols_term(lambda k=k: state[f"h{k}"], lambda: state.cot_cols), 1)
        elif kind == "up":
            make(tag, rows_term(lambda: mixed_of("second_pair"), lambda k=k: state[f"du{k}"]), 0)
        elif kind == "oo":
            make(tag, cols_term(piece_of(lambda: state.context, k, n), lambda: mixed_of("attn_pair")), 1)
        else:
            make(tag, rows_term(lambda: state.first_cols, piece_of(lambda: state.grad_query, k, n)), 0)

    def joined(kind, axis):
        found = sorted(name[:-2] for name in ORDER if name.startswith(kind) and name.endswith("_s"))
        return jnp.concatenate([state[tag] for tag in found], axis=axis)

    share = width // (n_d * n_t)

    @define(S.kv_m)
    def _():
        pair = over_tokens(hold(state.first_cols), state.kv_terms)
        term = (pair[:, : 2 * head_dim] + pair[:, 2 * head_dim :]).reshape(n_d, 2, 2, share, 2 * head_dim)
        core = t & 1
        sent = lax.dynamic_index_in_dim(term, 1 - core, 2, keepdims=False)
        state.kv_keep = lax.dynamic_index_in_dim(term, core, 2, keepdims=False)
        state.kv_c = swap(sent, "tensor", 1)
        done(sent)

    @define(S.kv_x)
    def _():
        total = state.kv_keep + hold(state.kv_c)
        chip = t >> 1
        sent = lax.dynamic_index_in_dim(total, 1 - chip, 1, keepdims=False)
        state.kv_keep = lax.dynamic_index_in_dim(total, chip, 1, keepdims=False)
        state.kv_xx = swap(sent, "tensor", 2)
        done(sent)

    @define(S.kv_s)
    def _():
        total = (state.kv_keep + hold(state.kv_xx)).reshape(n_d * share, 2 * head_dim)
        quart = n_d * share // 4
        state.kv_q1, state.kv_q0 = total[quart : 2 * quart], total[:quart]
        sent = total[2 * quart :]
        state.kv_y = swap(sent, "dp", 1)
        done(sent)

    @define(S.kv_q)
    def _():
        arrived = hold(state.kv_y)
        quart = n_d * share // 4
        sent = state.kv_q1 + arrived[:quart]
        state.kv_q0 = state.kv_q0 + arrived[quart:]
        state.kv_z1 = swap(sent, "dp", 2)
        done(sent)

    @define(S.kv_k)
    def _():
        total = state.kv_q0 + hold(state.kv_z1)
        kept, sent = tail(total, 0)
        state.kv_keep = kept
        state.kv_z2 = swap(sent, "dp", 4)
        done(total)

    @define(S.kv_f)
    def _():
        total = finish(state.kv_keep, hold(state.kv_z2), 0, 8)
        spread("kv", total, 0)
        done(total)

    pass_on("kv.g", "kv", 0)

    @define(S.kv_o)
    def _():
        own, other_x, other_c, other_cx = pieces_of("kv", 0)
        core, chip = t & 1, t >> 1
        pair = jnp.where(core == 0, jnp.stack([own, other_c]), jnp.stack([other_c, own]))
        pair_x = jnp.where(core == 0, jnp.stack([other_x, other_cx]), jnp.stack([other_cx, other_x]))
        whole = jnp.where(chip == 0, jnp.stack([pair, pair_x]), jnp.stack([pair_x, pair]))
        state.kv_grad = whole.reshape(n_t * share, 2 * head_dim)
        done(state.kv_grad)

    @define(S.v_0)
    def _():
        resid = jnp.concatenate([state[f"grad_resid{c}"] for c in range(PARTS)], axis=0)
        values = jnp.concatenate(
            [
                state.ln1_0[0] + state.ln1_1[0],
                state.ln1_0[1] + state.ln1_1[1],
                column_sum(resid.astype(BF16)),
                state.ln2_0[0] + state.ln2_1[0],
                state.ln2_0[1] + state.ln2_1[1],
                column_sum(own_cot),
                state.v_sum,
            ]
        )
        values = hold(values)
        state.v = values
        state.v_c = swap(values, "tensor", 1)
        done(values)

    @define(S.v_1)
    def _():
        state.v = state.v + hold(state.v_c)
        state.v_x = swap(state.v, "tensor", 2)
        done(state.v)

    @define(S.v_2)
    def _():
        total = state.v + hold(state.v_x)
        up_sum = state.up_sum
        state.v = jnp.concatenate([total, state.q_sum, up_sum])
        state.v_y = swap(state.v, "dp", 1)
        done(state.v)

    @define(S.v_3)
    def _():
        state.v = state.v + hold(state.v_y)
        state.v_z1 = swap(state.v, "dp", 2)
        done(state.v)

    @define(S.v_4)
    def _():
        state.v = state.v + hold(state.v_z1)
        state.v_z2 = swap(state.v, "dp", 4)
        done(state.v)

    @define(S.v_5)
    def _():
        total = state.v + hold(state.v_z2)
        bit = 8
        while bit < n_d:
            total = total + swap(total, "dp", bit)
            bit *= 2
        state.v = total
        done(total)

    for name in ORDER:
        with jax.named_scope("step." + name):
            steps[name]()

    vectors = []
    place = 0
    for size in (width,) * 6 + (head_dim, heads * head_dim, units):
        vectors.append(state.v[place : place + size])
        place += size
    return (
        jnp.concatenate([state.out0, state.out1], axis=0),
        state.input_grad,
        vectors[0],
        vectors[1],
        joined("qq", 1),
        vectors[7],
        state.kv_grad,
        vectors[6],
        joined("oo", 0),
        vectors[2],
        vectors[3],
        vectors[4],
        joined("up", 1),
        vectors[8],
        joined("dn", 0),
        vectors[5],
    )


def solution(mesh):
    in_specs = (
        P("dp", None),
        P("dp", None),
        P(),
        P(),
        P(None, "tensor"),
        P("tensor"),
        P(),
        P(),
        P("tensor", None),
        P(),
        P(),
        P(),
        P(None, "tensor"),
        P("tensor"),
        P("tensor", None),
        P(),
        P("dp", None),
    )
    out_specs = (
        P(("dp", "tensor"), None),
        P("dp", None),
        P(),
        P(),
        P("dp", "tensor"),
        P("tensor"),
        P("dp", None),
        P(),
        P("tensor", "dp"),
        P(),
        P(),
        P(),
        P("dp", "tensor"),
        P("tensor"),
        P("tensor", "dp"),
        P(),
    )
    return jax.shard_map(
        on_device, mesh=mesh, in_specs=in_specs, out_specs=out_specs, check_vma=False
    )
```

```python
from functools import partial

import jax
import jax.numpy as jnp
from jax import lax
from jax.experimental import pallas as pl
from jax.experimental.pallas import tpu as pltpu
from jax.sharding import PartitionSpec as P

EPS = 1e-05
F32 = jnp.float32
BF16 = jnp.bfloat16
CHUNKS = 4
PARTS = 2
LANES = 128

class Names:
    def __getattr__(self, name):
        return name


class Store(dict):
    __getattr__ = dict.__getitem__
    __setattr__ = dict.__setitem__


S = Names()

ORDER = (
    S.attn, S.ao_s0, S.ao_s1, S.ao_k0, S.cot, S.ao_k1, S.ao_a0, S.ao_a1, S.dh3, S.n0, S.dh2, S.a1p, S.dh1,
    S.n1, S.dh0, S.g0, S.g1, S.as0, S.as1, S.u0, S.dn04_s, S.up04_s, S.u1, S.u3, S.u2, S.join, S.ff_k1,
    S.sp_s1, S.sp_s0, S.dn04_q, S.dn34_s, S.sp_k1, S.sp_a1, S.ff_k0, S.sp_k0, S.dn04_k, S.sp_a0, S.b1,
    S.up04_q, S.dn04_f, S.up14_s, S.b0, S.up04_k, S.gb1, S.dn34_q, S.up04_f, S.dn24_s, S.gb0, S.asb1,
    S.dn34_k, S.ff_s0, S.up14_q, S.asb0, S.up24_s, S.abw, S.up14_k, S.dn24_q, S.dn34_f, S.fp_k0, S.qq12_s,
    S.ff_a0, S.fp_k1, S.up14_f, S.kv_m, S.dn24_k, S.up24_q, S.lo0, S.dn14_s, S.kv_x, S.dn24_f, S.fp_s1,
    S.up24_k, S.qq12_q, S.kv_s, S.fp_a1, S.qq12_k, S.kv_q, S.up24_f, S.up34_s, S.kv_k, S.dn14_q, S.qq12_f,
    S.oo01_s, S.kv_f, S.l1, S.kv_g0, S.dn14_k, S.kv_o, S.fp_s0, S.gl1, S.up34_q, S.dn14_f, S.qq02_s,
    S.fp_a0, S.up34_k, S.out1, S.oo01_q, S.l0, S.v_0, S.up34_f, S.ff_s1, S.oo01_k, S.v_1, S.gl0, S.qq02_q,
    S.v_2, S.ff_a1, S.qq02_k, S.oo01_f, S.v_3, S.out0, S.qq02_f, S.v_4, S.lo1, S.v_5,
)


def reverse_bits(value, n):
    bits = n.bit_length() - 1
    assert 1 << bits == n
    out = 0
    for b in range(bits):
        out = out | (((value >> b) & 1) << (bits - 1 - b))
    return out


def quarter_order(n):
    rest = n // 4
    return [low + 4 * reverse_bits(i, rest) for low in (0, 2, 3, 1) for i in range(rest)]


def swap(values, axis_name, bit):
    n = lax.axis_size(axis_name)
    return lax.ppermute(values, axis_name, [(i, i ^ bit) for i in range(n)])


def layer_norm(values):
    mean_row = jnp.mean(values, axis=-1, keepdims=True)
    centred = values - mean_row
    inv_scale = lax.rsqrt(jnp.mean(centred * centred, axis=-1, keepdims=True) + EPS)
    return (centred * inv_scale, inv_scale)


def norm_back(grad_out, normed, inv_scale, gain):
    scaled = grad_out * gain
    inner = (
        scaled
        - jnp.mean(scaled, axis=-1, keepdims=True)
        - normed * jnp.mean(scaled * normed, axis=-1, keepdims=True)
    )
    return (inner * inv_scale, jnp.sum(grad_out * normed, axis=0), jnp.sum(grad_out, axis=0))


def visible_mask(ids_win, start, finish):
    query_pos = start + jnp.arange(finish - start)
    key_pos = jnp.arange(finish)
    same_doc = ids_win[start:finish][:, None] == ids_win[:finish][None, :]
    return (key_pos[None, :] <= query_pos[:, None]) & same_doc


def attend_window(q_win, k_win, v_win, ids_win):
    length = ids_win.shape[0]
    block = min(512, length)
    factor = q_win.shape[-1] ** (-0.5)
    outs = []
    sums = []
    for start in range(0, length, block):
        finish = start + block
        scores = (
            jnp.einsum("qhd,kd->hqk", q_win[start:finish], k_win[:finish], preferred_element_type=F32)
            * factor
        )
        visible = visible_mask(ids_win, start, finish)
        scores = jnp.where(visible[None], scores, -1e30)
        peak = jnp.max(scores, axis=-1, keepdims=True)
        expo = jnp.exp(scores - peak)
        total = jnp.sum(expo, axis=-1, keepdims=True)
        probs = (expo / total).astype(BF16)
        outs.append(jnp.einsum("hqk,kd->qhd", probs, v_win[:finish], preferred_element_type=F32))
        sums.append((peak + jnp.log(total))[..., 0])
    return (jnp.concatenate(outs, axis=0), jnp.concatenate(sums, axis=1))


def attend_back(q_win, k_win, v_win, ids_win, lse_win, grad_win):
    length = ids_win.shape[0]
    head_dim = k_win.shape[-1]
    block = min(512, length)
    factor = head_dim ** (-0.5)
    grad_q_parts = []
    grad_keys = jnp.zeros((length, head_dim), F32)
    grad_vals = jnp.zeros((length, head_dim), F32)
    for start in range(0, length, block):
        finish = start + block
        q_part = q_win[start:finish]
        grad_part = grad_win[start:finish]
        scores = (
            jnp.einsum("qhd,kd->hqk", q_part, k_win[:finish], preferred_element_type=F32) * factor
        )
        visible = visible_mask(ids_win, start, finish)
        probs = jnp.where(visible[None], jnp.exp(scores - lse_win[:, start:finish, None]), 0.0)
        grad_probs = jnp.einsum("qhd,kd->hqk", grad_part, v_win[:finish], preferred_element_type=F32)
        grad_vals = grad_vals.at[:finish].add(
            jnp.einsum("hqk,qhd->kd", probs.astype(BF16), grad_part, preferred_element_type=F32)
        )
        delta = jnp.sum(probs * grad_probs, axis=-1, keepdims=True)
        grad_scores = (probs * (grad_probs - delta)).astype(BF16)
        grad_q_parts.append(
            jnp.einsum("hqk,kd->qhd", grad_scores, k_win[:finish], preferred_element_type=F32) * factor
        )
        grad_keys = grad_keys.at[:finish].add(
            jnp.einsum("hqk,qhd->kd", grad_scores, q_part, preferred_element_type=F32) * factor
        )
    return (jnp.concatenate(grad_q_parts, axis=0), grad_keys, grad_vals)


def over_tokens(left, right):
    return jnp.einsum("tf,td->fd", left, right, preferred_element_type=F32)


def back_term(grad, weight):
    return jnp.einsum("td,fd->tf", grad, weight, preferred_element_type=F32)


def forward_term(values, weight):
    return jnp.dot(values, weight, preferred_element_type=F32)


def column_sum(values):
    return jnp.sum(values.astype(F32), axis=0)


def mix_columns(values, spots, n):
    size = values.shape[1] // n
    return jnp.take(values, (spots[:, None] * size + jnp.arange(size)[None, :]).reshape(-1), axis=1)


def arrange(values, row_spots, col_spots, plain, mixed):
    n_rows, n_cols = row_spots.shape[0], col_spots.shape[0]
    height, width = values.shape[0] // n_rows, values.shape[1]
    size = width // n_cols
    if mixed and size % LANES:
        both = arrange(values, row_spots, col_spots, True, False)
        mix = (mix_columns(both[0], col_spots, n_cols),)
        return both + mix if plain else mix
    fan = n_rows // 2 if width * height * n_rows > (1 << 20) else n_rows

    def body(rows, cols, *refs):
        ins, outs = refs[:fan], list(refs[fan:])
        if plain:
            out = outs.pop(0)
            for k in range(fan):
                out[k * height : (k + 1) * height, :] = ins[k][...]
        if mixed:
            out = outs.pop(0)
            for k in range(fan):
                for p in range(n_cols):
                    place = pl.multiple_of(cols[p] * size, LANES)
                    out[k * height : (k + 1) * height, p * size : (p + 1) * size] = ins[k][:, pl.ds(place, size)]

    count = int(plain) + int(mixed)
    out = pl.pallas_call(
        body,
        out_shape=[jax.ShapeDtypeStruct(values.shape, values.dtype)] * count,
        grid_spec=pltpu.PrefetchScalarGridSpec(
            num_scalar_prefetch=2,
            grid=(n_rows // fan,),
            in_specs=[
                pl.BlockSpec((height, width), lambda i, rows, cols, k=k: (rows[i * fan + k], 0))
                for k in range(fan)
            ],
            out_specs=[pl.BlockSpec((fan * height, width), lambda i, rows, cols: (i, 0))] * count,
        ),
        name="arrange",
    )(row_spots, col_spots, *([values] * fan))
    return tuple(out)


def take_in(pieces, shared, part, col_spots, combine, earlier):
    own, other, both = pieces
    count = 4
    height, width = own.shape
    n_cols = col_spots.shape[0]
    size = width // n_cols
    mixing = size % LANES == 0
    outputs = 2 if mixing else 1
    strip = height // 4

    def body(cols, *refs):
        ins, rest = refs[:count], refs[count:]
        extra = rest[: len(shared)]
        outs = rest[len(rest) - outputs :]
        for p in range(count):
            block = [e[0, p] if len(e.shape) == 4 else e[...] for e in extra]
            outs[0][0, p] = combine(ins[p][...], *block).astype(BF16)
            if mixing:
                for k in range(n_cols):
                    place = pl.multiple_of(cols[k] * size, LANES)
                    outs[1][0, p, :, k * size : (k + 1) * size] = outs[0][0, p, :, pl.ds(place, size)]

    rows_block = pl.BlockSpec((1, count, strip, width), lambda i, cols: (part, 0, i, 0))
    in_specs = [
        pl.BlockSpec((strip, width), lambda i, cols, low=low: (i + low, 0)) for low in (0, 0, 0, height // strip)
    ]
    operands = [own, other, both, both]
    for s in shared:
        if s.shape[0] == 1:
            in_specs.append(pl.BlockSpec((1, width), lambda i, cols: (0, 0)))
            operands.append(s)
        else:
            in_specs.append(rows_block)
            operands.append(s.reshape(PARTS, count, height, width))
    aliases = {}
    if earlier is not None:
        for k in range(outputs):
            aliases[1 + len(operands)] = k
            operands.append(earlier[k].reshape(PARTS, count, height, width))
            in_specs.append(pl.BlockSpec(memory_space=pl.ANY))
    out = pl.pallas_call(
        body,
        out_shape=[jax.ShapeDtypeStruct((PARTS, count, height, width), BF16)] * outputs,
        grid_spec=pltpu.PrefetchScalarGridSpec(
            num_scalar_prefetch=1,
            grid=(height // strip,),
            in_specs=in_specs,
            out_specs=[rows_block] * outputs,
        ),
        input_output_aliases=aliases,
        name="take_in",
    )(col_spots, *operands)
    return tuple(o.reshape(PARTS * count * height, width) for o in out), out[0]


def place_rows(pieces, row_spots, total_rows, earlier):
    own, other, both = pieces
    count = 4
    height, width = own.shape

    def body(rows, *refs):
        i = pl.program_id(0)
        for p in range(count):

            @pl.when(i == p)
            def _():
                refs[-1][...] = refs[p][...]

    operands = [own, other, both, both]
    in_specs = [pl.BlockSpec((height, width), lambda i, rows, low=low: (low, 0)) for low in (0, 0, 0, 1)]
    aliases = {}
    if earlier is not None:
        aliases[1 + count] = 0
        operands.append(earlier)
        in_specs.append(pl.BlockSpec(memory_space=pl.ANY))
    return pl.pallas_call(
        body,
        out_shape=jax.ShapeDtypeStruct((total_rows, width), F32),
        grid_spec=pltpu.PrefetchScalarGridSpec(
            num_scalar_prefetch=1,
            grid=(count,),
            in_specs=in_specs,
            out_specs=pl.BlockSpec((height, width), lambda i, rows: (rows[i], 0)),
        ),
        input_output_aliases=aliases,
        name="place_rows",
    )(row_spots, *operands)


def on_device(
    hidden_in,
    doc_ids,
    ln1_gain,
    ln1_bias,
    q_weight,
    q_bias,
    kv_weight,
    v_bias,
    o_weight,
    o_bias,
    ln2_gain,
    ln2_bias,
    up_weight,
    up_bias,
    down_weight,
    down_bias,
    cotangent,
):
    n_t = lax.axis_size("tensor")
    n_d = lax.axis_size("dp")
    assert n_t == 4 and n_d >= 4
    t = lax.axis_index("tensor")
    d = lax.axis_index("dp")
    rows_here, width = hidden_in.shape
    windows, length = doc_ids.shape
    head_dim = kv_weight.shape[1] // 2
    heads = q_weight.shape[1] // head_dim
    units = up_weight.shape[1]
    own_rows = rows_here // n_t
    piece = own_rows // PARTS
    part_rows = rows_here // PARTS

    t_order = [reverse_bits(p, n_t) for p in range(n_t)]
    part_spots = [jnp.stack([(t ^ k) * PARTS + c for k in t_order]).astype(jnp.int32) for c in range(PARTS)]
    row_spots = jnp.concatenate(part_spots)
    row_back = jnp.stack(
        [c * n_t + reverse_bits(t ^ j, n_t) for j in range(n_t) for c in range(PARTS)]
    ).astype(jnp.int32)
    row_same = jnp.arange(n_t * PARTS, dtype=jnp.int32)
    col_spots = jnp.stack([d ^ k for k in quarter_order(n_d)]).astype(jnp.int32)

    state = Store()
    steps = {}
    last = []

    def define(name):
        def put(fn):
            steps[name.replace(".", "_")] = fn
            return fn

        return put

    def hold(*values):
        if not last:
            return values if len(values) > 1 else values[0]
        out = lax.optimization_barrier(tuple(values) + (last[-1],))
        return out[:-1] if len(values) > 1 else out[0]

    def done(value):
        last[:] = [value]

    def part_of(values, c):
        return values[c * part_rows : (c + 1) * part_rows]

    @define(S.attn)
    def _():
        normed, _ = layer_norm(hidden_in.astype(F32))
        first_in = (normed * ln1_gain + ln1_bias).astype(BF16)
        queries = (forward_term(first_in, q_weight) + q_bias).astype(BF16)
        kv_shift = jnp.concatenate([jnp.zeros((head_dim,), F32), v_bias.astype(F32)])
        keyvals = (forward_term(first_in, kv_weight) + kv_shift).astype(BF16)
        q_all = queries.reshape(windows, length, heads, head_dim)
        k_all = keyvals[:, :head_dim].reshape(windows, length, head_dim)
        v_all = keyvals[:, head_dim:].reshape(windows, length, head_dim)
        attended = [attend_window(q_all[w], k_all[w], v_all[w], doc_ids[w]) for w in range(windows)]
        context = jnp.concatenate([a[0].reshape(length, heads * head_dim) for a in attended], axis=0)
        context = arrange(context.astype(BF16), row_spots, col_spots, True, False)[0]
        state.update(first_in=first_in, q=q_all, k=k_all, v=v_all, lse=[a[1] for a in attended])
        state.update(context=context)
        done(context)

    @define(S.cot)
    def _():
        state.cot, state.cot_cols = arrange(hold(cotangent), row_spots, col_spots, True, True)
        done(state.cot_cols)

    unit_step = units // CHUNKS

    for k in range(CHUNKS):
        here = slice(k * unit_step, (k + 1) * unit_step)

        @define(f"dh{k}")
        def _(k=k, here=here):
            state[f"dh{k}"] = back_term(hold(state.cot), down_weight[here])
            done(state[f"dh{k}"])

        @define(f"u{k}")
        def _(k=k, here=here):
            second = hold(state.second_pair[0])
            upper = forward_term(second, up_weight[:, here]) + up_bias[here]
            value, pull = jax.vjp(partial(jax.nn.gelu, approximate=True), upper)
            state[f"h{k}"] = value.astype(BF16)
            state[f"du{k}"] = pull(state[f"dh{k}"])[0].astype(BF16)
            done(state[f"h{k}"])

    @define(S.join)
    def _():
        parts = hold(*[state[f"{name}{k}"] for name in ("h", "du") for k in range(CHUNKS)])
        state.activ = jnp.concatenate(parts[:CHUNKS], axis=1)
        state.grad_upper = jnp.concatenate(parts[CHUNKS:], axis=1)
        state.up_sum = column_sum(state.grad_upper)
        done(state.grad_upper)

    @define(S.a1p)
    def _():
        state.first_cols = arrange(hold(state.first_in), row_same, col_spots, False, True)[0]
        done(state.first_cols)

    def row_sum(tag, values, multiply, c):
        low = c * part_rows
        middle = low + part_rows // 2

        @define(f"{tag}_s{c}")
        def _():
            sent = multiply(hold(values()[middle : middle + part_rows // 2]))
            state[f"{tag}_c{c}"] = swap(sent, "tensor", 1)
            done(sent)

        @define(f"{tag}_k{c}")
        def _():
            total = multiply(hold(values()[low:middle]))
            state[f"{tag}_kept{c}"] = total
            done(total)

        @define(f"{tag}_a{c}")
        def _():
            arrived = hold(state[f"{tag}_c{c}"])
            kept = state[f"{tag}_kept{c}"]
            sent = kept[piece:] + arrived[piece:]
            state[f"{tag}_near{c}"] = arrived
            state[f"{tag}_x{c}"] = swap(sent, "tensor", 2)
            done(sent)

    def own_sum(tag, c):
        arrived = hold(state[f"{tag}_x{c}"])
        return state[f"{tag}_kept{c}"][:piece] + state[f"{tag}_near{c}"][:piece] + arrived

    def spread(tag, values, c):
        state[f"{tag}{c}"] = values
        state[f"{tag}x{c}"] = swap(values, "tensor", 2)

    def pass_on(name, tag, c):
        @define(f"{name}{c}")
        def _():
            arrived = hold(state[f"{tag}x{c}"])
            state[f"{tag}x{c}"] = arrived
            both = jnp.concatenate([state[f"{tag}{c}"], arrived], axis=0)
            state[f"{tag}g{c}"] = swap(both, "tensor", 1)
            done(both)

    def pieces_of(tag, c):
        return hold(state[f"{tag}{c}"], state[f"{tag}x{c}"], state[f"{tag}g{c}"])

    own_in = lax.dynamic_slice_in_dim(hidden_in, t * own_rows, own_rows, 0)
    own_cot = lax.dynamic_slice_in_dim(cotangent, t * own_rows, own_rows, 0)

    def own_part(values, c):
        return values[c * piece : (c + 1) * piece].astype(F32)

    for c in range(PARTS):
        row_sum("ao", lambda: state.context, lambda v: forward_term(v, o_weight), c)

        @define(f"n{c}")
        def _(c=c):
            resid = own_part(own_in, c) + own_sum("ao", c) + o_bias
            plain, scale = layer_norm(resid)
            state[f"resid{c}"] = resid
            state[f"scale{c}"] = scale
            spread("n", plain, c)
            done(plain)

        pass_on("g", "n", c)

        @define(f"as{c}")
        def _(c=c):
            out, token = take_in(
                pieces_of("n", c),
                [ln2_gain.reshape(1, width), ln2_bias.reshape(1, width)],
                c,
                col_spots,
                lambda v, g, b: v * g.astype(F32) + b.astype(F32),
                state.get(S.second_pair),
            )
            state.second_pair = out
            done(token)

        row_sum("sp", lambda: state.grad_upper, lambda v: back_term(v, up_weight), c)
        row_sum("ff", lambda: state.activ, lambda v: forward_term(v, down_weight), c)

        @define(f"lo{c}")
        def _(c=c):
            state[f"out{c}"] = (state[f"resid{c}"] + own_sum("ff", c) + down_bias).astype(BF16)
            done(state[f"out{c}"])

        @define(f"b{c}")
        def _(c=c):
            grad_second = own_sum("sp", c)
            back, gain_grad, bias_grad = norm_back(
                grad_second, state[f"n{c}"], state[f"scale{c}"], ln2_gain
            )
            spread("b", back, c)
            state[f"grad_resid{c}"] = own_part(own_cot, c) + back
            state[f"ln2_{c}"] = (gain_grad, bias_grad)
            done(back)

        pass_on("gb", "b", c)

        @define(f"asb{c}")
        def _(c=c):
            out, token = take_in(
                pieces_of("b", c),
                [state.cot],
                c,
                col_spots,
                lambda v, g: g.astype(F32) + v,
                state.get(S.attn_pair),
            )
            state.attn_pair = out
            done(token)

        row_sum("fp", lambda: state.stack, lambda v: back_term(v, state.stack_w), c)

        @define(f"l{c}")
        def _(c=c):
            grad_first = own_sum("fp", c)
            plain, scale = layer_norm(own_part(own_in, c))
            back, gain_grad, bias_grad = norm_back(grad_first, plain, scale, ln1_gain)
            result = state[f"grad_resid{c}"] + back
            spread("l", result, c)
            state[f"ln1_{c}"] = (gain_grad, bias_grad)
            done(result)

        pass_on("gl", "l", c)

        @define(f"out{c}")
        def _(c=c):
            out = place_rows(pieces_of("l", c), part_spots[c], rows_here, state.get(S.input_grad))
            state.input_grad = out
            done(out)

    @define(S.abw)
    def _():
        grad_attn = hold(state.attn_pair[0])
        grad_context = back_term(grad_attn, o_weight).astype(BF16)
        grad_context = arrange(grad_context, row_back, col_spots, True, False)[0]
        grad_ctx_all = grad_context.reshape(windows, length, heads, head_dim)
        pulled = [
            attend_back(state.q[w], state.k[w], state.v[w], doc_ids[w], state.lse[w], grad_ctx_all[w])
            for w in range(windows)
        ]
        grad_query = jnp.concatenate(
            [p[0].reshape(length, heads * head_dim) for p in pulled], axis=0
        ).astype(BF16)
        kv_part = jnp.concatenate([jnp.concatenate([p[1], p[2]], axis=-1) for p in pulled], axis=0)
        high = kv_part.astype(BF16)
        low = (kv_part - high.astype(F32)).astype(BF16)
        stack = jnp.concatenate([grad_query, high, low], axis=1)
        state.grad_query = grad_query
        state.kv_terms = jnp.concatenate([high, low], axis=1)
        state.q_sum = column_sum(grad_query)
        state.v_sum = jnp.sum(kv_part[:, head_dim:], axis=0)
        state.stack = arrange(stack, row_spots, col_spots, True, False)[0]
        state.stack_w = jnp.concatenate([q_weight, kv_weight, kv_weight], axis=1)
        done(state.stack)

    half = width // 2
    quarter = width // 4

    def cut(values, lo, hi, axis):
        return lax.slice_in_dim(values, lo, hi, axis=axis)

    def tail(values, axis):
        middle = values.shape[axis] // 2
        return cut(values, 0, middle, axis), cut(values, middle, 2 * middle, axis)

    def finish(kept, sent_back, axis, bit):
        total = kept + sent_back
        while bit < n_d:
            kept, sent = tail(total, axis)
            total = kept + swap(sent, "dp", bit)
            bit *= 2
        return total

    def dims(axis, block, other):
        return (block, other) if axis == 0 else (other, block)

    def grad_low_first(tag, term, axis):
        @define(f"{tag}.s")
        def _():
            sent = term(half, width, hold)
            state[f"{tag}.y"] = swap(sent, "dp", 1)
            done(sent)

        @define(f"{tag}.q")
        def _():
            arrived = hold(state[f"{tag}.y"])
            total = term(quarter, half, lambda v: v) + cut(arrived, 0, quarter, axis)
            state[f"{tag}.rest"] = cut(arrived, quarter, half, axis)
            state[f"{tag}.z1"] = swap(total, "dp", 2)
            done(total)

        @define(f"{tag}.k")
        def _():
            arrived, rest = hold(state[f"{tag}.z1"], state[f"{tag}.rest"])
            total = term(0, quarter, lambda v: v) + rest + arrived
            kept, sent = tail(total, axis)
            state[f"{tag}.kept"] = kept
            state[f"{tag}.z2"] = swap(sent, "dp", 4)
            done(total)

        @define(f"{tag}.f")
        def _():
            arrived = hold(state[f"{tag}.z2"])
            state[tag] = finish(state[f"{tag}.kept"], arrived, axis, 8)
            done(state[tag])

    def grad_high_first(tag, term, axis):
        @define(f"{tag}.s")
        def _():
            sent = term(quarter, 3 * quarter, hold)
            state[f"{tag}.z1"] = swap(sent, "dp", 2)
            done(sent)

        @define(f"{tag}.q")
        def _():
            arrived = hold(state[f"{tag}.z1"])
            near = term(0, quarter, lambda v: v) + cut(arrived, 0, quarter, axis)
            far = term(3 * quarter, width, lambda v: v) + cut(arrived, quarter, half, axis)
            near, near_sent = tail(near, axis)
            far, far_sent = tail(far, axis)
            sent = jnp.concatenate([near_sent, far_sent], axis=axis)
            state[f"{tag}.kept"] = (near, far)
            state[f"{tag}.z2"] = swap(sent, "dp", 4)
            done(sent)

        @define(f"{tag}.k")
        def _():
            arrived = hold(state[f"{tag}.z2"])
            near, far = state[f"{tag}.kept"]
            a, b = tail(arrived, axis)
            near = finish(near, a, axis, 8)
            far = finish(far, b, axis, 8)
            state[f"{tag}.kept"] = near
            state[f"{tag}.y"] = swap(far, "dp", 1)
            done(far)

        @define(f"{tag}.f")
        def _():
            arrived = hold(state[f"{tag}.y"])
            state[tag] = state[f"{tag}.kept"] + arrived
            done(state[tag])

    def mixed_of(pair_name):
        pair = state[pair_name]
        return pair[1] if len(pair) > 1 else mix_columns(pair[0], col_spots, n_d)

    def rows_term(left, right):
        def term(lo, hi, h):
            return over_tokens(h(left()[:, lo:hi]), right())

        return term

    def cols_term(left, right):
        def term(lo, hi, h):
            return over_tokens(left(), h(right()[:, lo:hi]))

        return term

    def piece_of(get, k, n):
        def f():
            values = get()
            size = values.shape[1] // n
            return values[:, k * size : (k + 1) * size]

        return f

    for name in ORDER:
        if not name.endswith("_s") or name.startswith("kv"):
            continue
        tag = name[:-2]
        kind, index = tag[:2], tag[2:]
        k, n, high = int(index[0]), int(index[1]), index.endswith("z")
        make = grad_high_first if high else grad_low_first
        if kind == "dn":
            make(tag, cols_term(lambda k=k: state[f"h{k}"], lambda: state.cot_cols), 1)
        elif kind == "up":
            make(tag, rows_term(lambda: mixed_of("second_pair"), lambda k=k: state[f"du{k}"]), 0)
        elif kind == "oo":
            make(tag, cols_term(piece_of(lambda: state.context, k, n), lambda: mixed_of("attn_pair")), 1)
        else:
            make(tag, rows_term(lambda: state.first_cols, piece_of(lambda: state.grad_query, k, n)), 0)

    def joined(kind, axis):
        found = sorted(name[:-2] for name in ORDER if name.startswith(kind) and name.endswith("_s"))
        return jnp.concatenate([state[tag] for tag in found], axis=axis)

    share = width // (n_d * n_t)

    @define(S.kv_m)
    def _():
        pair = over_tokens(hold(state.first_cols), state.kv_terms)
        term = (pair[:, : 2 * head_dim] + pair[:, 2 * head_dim :]).reshape(n_d, 2, 2, share, 2 * head_dim)
        core = t & 1
        sent = lax.dynamic_index_in_dim(term, 1 - core, 2, keepdims=False)
        state.kv_keep = lax.dynamic_index_in_dim(term, core, 2, keepdims=False)
        state.kv_c = swap(sent, "tensor", 1)
        done(sent)

    @define(S.kv_x)
    def _():
        total = state.kv_keep + hold(state.kv_c)
        chip = t >> 1
        sent = lax.dynamic_index_in_dim(total, 1 - chip, 1, keepdims=False)
        state.kv_keep = lax.dynamic_index_in_dim(total, chip, 1, keepdims=False)
        state.kv_xx = swap(sent, "tensor", 2)
        done(sent)

    @define(S.kv_s)
    def _():
        total = (state.kv_keep + hold(state.kv_xx)).reshape(n_d * share, 2 * head_dim)
        quart = n_d * share // 4
        state.kv_q1, state.kv_q0 = total[quart : 2 * quart], total[:quart]
        sent = total[2 * quart :]
        state.kv_y = swap(sent, "dp", 1)
        done(sent)

    @define(S.kv_q)
    def _():
        arrived = hold(state.kv_y)
        quart = n_d * share // 4
        sent = state.kv_q1 + arrived[:quart]
        state.kv_q0 = state.kv_q0 + arrived[quart:]
        state.kv_z1 = swap(sent, "dp", 2)
        done(sent)

    @define(S.kv_k)
    def _():
        total = state.kv_q0 + hold(state.kv_z1)
        kept, sent = tail(total, 0)
        state.kv_keep = kept
        state.kv_z2 = swap(sent, "dp", 4)
        done(total)

    @define(S.kv_f)
    def _():
        total = finish(state.kv_keep, hold(state.kv_z2), 0, 8)
        spread("kv", total, 0)
        done(total)

    pass_on("kv.g", "kv", 0)

    @define(S.kv_o)
    def _():
        own, other_x, both = pieces_of("kv", 0)
        other_c, other_cx = both[:own.shape[0]], both[own.shape[0]:]
        core, chip = t & 1, t >> 1
        pair = jnp.where(core == 0, jnp.stack([own, other_c]), jnp.stack([other_c, own]))
        pair_x = jnp.where(core == 0, jnp.stack([other_x, other_cx]), jnp.stack([other_cx, other_x]))
        whole = jnp.where(chip == 0, jnp.stack([pair, pair_x]), jnp.stack([pair_x, pair]))
        state.kv_grad = whole.reshape(n_t * share, 2 * head_dim)
        done(state.kv_grad)

    @define(S.v_0)
    def _():
        resid = jnp.concatenate([state[f"grad_resid{c}"] for c in range(PARTS)], axis=0)
        values = jnp.concatenate(
            [
                state.ln1_0[0] + state.ln1_1[0],
                state.ln1_0[1] + state.ln1_1[1],
                column_sum(resid.astype(BF16)),
                state.ln2_0[0] + state.ln2_1[0],
                state.ln2_0[1] + state.ln2_1[1],
                column_sum(own_cot),
                state.v_sum,
            ]
        )
        values = hold(values)
        state.v = values
        state.v_c = swap(values, "tensor", 1)
        done(values)

    @define(S.v_1)
    def _():
        state.v = state.v + hold(state.v_c)
        state.v_x = swap(state.v, "tensor", 2)
        done(state.v)

    @define(S.v_2)
    def _():
        total = state.v + hold(state.v_x)
        up_sum = state.up_sum
        state.v = jnp.concatenate([total, state.q_sum, up_sum])
        state.v_y = swap(state.v, "dp", 1)
        done(state.v)

    @define(S.v_3)
    def _():
        state.v = state.v + hold(state.v_y)
        state.v_z1 = swap(state.v, "dp", 2)
        done(state.v)

    @define(S.v_4)
    def _():
        state.v = state.v + hold(state.v_z1)
        state.v_z2 = swap(state.v, "dp", 4)
        done(state.v)

    @define(S.v_5)
    def _():
        total = state.v + hold(state.v_z2)
        bit = 8
        while bit < n_d:
            total = total + swap(total, "dp", bit)
            bit *= 2
        state.v = total
        done(total)

    for name in ORDER:
        with jax.named_scope("step." + name):
            steps[name]()

    vectors = []
    place = 0
    for size in (width,) * 6 + (head_dim, heads * head_dim, units):
        vectors.append(state.v[place : place + size])
        place += size
    return (
        jnp.concatenate([state.out0, state.out1], axis=0),
        state.input_grad,
        vectors[0],
        vectors[1],
        joined("qq", 1),
        vectors[7],
        state.kv_grad,
        vectors[6],
        joined("oo", 0),
        vectors[2],
        vectors[3],
        vectors[4],
        joined("up", 1),
        vectors[8],
        joined("dn", 0),
        vectors[5],
    )


def solution(mesh):
    in_specs = (
        P("dp", None),
        P("dp", None),
        P(),
        P(),
        P(None, "tensor"),
        P("tensor"),
        P(),
        P(),
        P("tensor", None),
        P(),
        P(),
        P(),
        P(None, "tensor"),
        P("tensor"),
        P("tensor", None),
        P(),
        P("dp", None),
    )
    out_specs = (
        P(("dp", "tensor"), None),
        P("dp", None),
        P(),
        P(),
        P("dp", "tensor"),
        P("tensor"),
        P("dp", None),
        P(),
        P("tensor", "dp"),
        P(),
        P(),
        P(),
        P("dp", "tensor"),
        P("tensor"),
        P("tensor", "dp"),
        P(),
    )
    return jax.shard_map(
        on_device, mesh=mesh, in_specs=in_specs, out_specs=out_specs, check_vma=False
    )
```
